512 devices in a mesh: dp: 8 (over y, core), expert: 64 (over z, x).
Axes of the slice: x: 4, y: 4, z: 16, core: 2. Of those that a mesh axis runs over, the one named last changes fastest.
Arguments:
- latent: bfloat16 [65536, 4096], P(('dp', 'expert')), may hold values from -6 to 6
- dout: bfloat16 [65536, 4096], P(('dp', 'expert')), may hold values from -6 to 6
- routes: int32 [65536, 2], P(('dp', 'expert')), may hold values from 0 to 63, as said below
- gate_w: float32 [65536, 2], P(('dp', 'expert')), may hold values from 0.1 to 1
- norm_gain: float32 [4096], replicated, may hold values from 0.1 to 1.9
- w_gate_up: bfloat16 [64, 4096, 256], P('expert', 'dp'), may hold values from -0.09375 to 0.09375
- w_down: bfloat16 [64, 128, 4096], P('expert', None, 'dp'), may hold values from -0.1875 to 0.1875
Outputs:
- d_latent: bfloat16 [65536, 4096], P(('dp', 'expert'))
- grad_gate_up: bfloat16 [64, 4096, 256], P('expert', 'dp')
- grad_down: bfloat16 [64, 128, 4096], P('expert', None, 'dp')
The draws below stay inside these ranges and needn't reach their ends.
Inputs may be any that keep to these rules, and one draw needn't show every extreme that they name: `routes`: each patch names two different experts, at most one of them below 8. The patches of one device name no expert below 8 more than 4 times, and in every draw some expert below 8 is named exactly 4 times by the patches of every device of one index of dp.
All inputs are finite; a program needn't handle non-finite values.
Results may differ from the reference program's by a relative error of at most 0.013.
Values may be sent and summed in bfloat16 or wider, within the bound.
No kernel may reach another device: no remote copies, remote signals or barrier semaphores. Data moves between devices by JAX's collectives and lax.ppermute only.
A program may use at most 64 MiB of HBM per device.

```python
import jax
import jax.numpy as jnp
from jax import lax

D = 4096
H = 1024
EXPERTS = 64
SLICES = 8
CAP = 4
P_DEV = 128
HID_DEV = 128
E_FL = 8
SLOTS = 64
TOKENS = 65536
N_DP = 8
N_EXPERT = 64


def draw_routes(key, part):
    blocks = N_DP * N_EXPERT
    keys = jax.random.split(key, 6)
    hot = jax.random.randint(keys[0], (N_DP,), 0, E_FL)
    hot_block = jnp.repeat(hot, N_EXPERT, total_repeat_length=blocks)
    counts = jax.random.randint(keys[1], (blocks, E_FL), 0, CAP // 2 + 1)
    counts = jnp.where(jnp.arange(E_FL)[None, :] == hot_block[:, None], CAP, counts)
    ends = jnp.cumsum(counts, axis=1)
    order = jax.vmap(lambda one: jax.random.permutation(one, P_DEV))(jax.random.split(keys[2], blocks))
    first = jnp.sum((order[:, :, None] >= ends[:, None, :]).astype(jnp.int32), axis=2)
    outside = jax.random.randint(keys[3], (blocks, P_DEV), E_FL, EXPERTS)
    first = jnp.where(first < E_FL, first, outside)
    raw = jax.random.randint(keys[4], (blocks, P_DEV), E_FL, EXPERTS - 1)
    second = jnp.where((first >= E_FL) & (raw >= first), raw + 1, raw)
    flip = jax.random.randint(keys[5], (blocks, P_DEV), 0, 2) == 1
    left = jnp.where(flip, second, first)
    right = jnp.where(flip, first, second)
    return jnp.stack([left, right], axis=2).reshape(blocks * P_DEV, 2).astype(jnp.int32)


def steps_of(rng, extent, shards, low, top_value):
    def one(dim, shards_of):
        steps = jax.random.uniform(jax.random.fold_in(jax.random.fold_in(rng, 6), dim), (shards_of,), jnp.float32, low / len(shards), top_value / len(shards))
        return jnp.repeat(jnp.exp(steps), extent[dim] // shards_of).reshape((-1,) + (1,) * (len(extent) - dim - 1))

    loudness = one(*shards[0])
    for cut in shards[1:]:
        loudness = loudness * one(*cut)
    return loudness


def scatter_about(rng, shape, scale, bound, pieces=(), kind=jnp.bfloat16):
    entries = scale * jax.random.normal(rng, shape, jnp.float32)
    if pieces:
        entries = entries * steps_of(rng, shape, pieces, -0.22, 0.18)
    return jnp.clip(entries, -bound, bound).astype(kind)


def setup_inputs(seed: int = 0) -> dict:
    splits = jax.random.split(jax.random.key(seed), 8)
    return {
        "latent": scatter_about(splits[0], (TOKENS, D), 1.0, 6.0, ((0, 512),)),
        "dout": scatter_about(splits[1], (TOKENS, D), 1.0, 6.0, ((0, 512),)),
        "routes": draw_routes(jax.random.fold_in(splits[7], 71), 0),
        "gate_w": jnp.clip(0.1 + 0.9 * jax.random.uniform(splits[3], (TOKENS, 2), jnp.float32) ** steps_of(splits[3], (TOKENS, 2), ((0, 512),), -0.2, 0.2), 0.1, 1.0),
        "norm_gain": jnp.clip(1.0 + 0.18 * jax.random.normal(splits[4], (D,), jnp.float32), 0.1, 1.9),
        "w_gate_up": scatter_about(splits[5], (SLOTS, D, 2 * HID_DEV), D ** -0.5, 0.09375, ((0, 64), (1, 8))),
        "w_down": scatter_about(splits[6], (SLOTS, HID_DEV, D), H ** -0.5, 0.1875, ((0, 64), (2, 8))),
    }


EPS = 1e-06

def expert_pass(rows_in, rows_dy, wgu, wd):
    hid = wd.shape[0]
    pre = jnp.dot(rows_in, wgu, preferred_element_type=jnp.float32)
    gate = pre[:, :hid]
    up = pre[:, hid:]
    sig = jax.nn.sigmoid(gate)
    act = gate * sig
    hidden = (act * up).astype(jnp.bfloat16)
    dh = jnp.dot(rows_dy, wd.T, preferred_element_type=jnp.float32)
    d_up = dh * act
    d_gate = dh * up * sig * (1.0 + gate * (1.0 - sig))
    d_pre = jnp.concatenate([d_gate, d_up], axis=1).astype(jnp.bfloat16)
    return (hidden, d_pre)

def group_work(xe, ye, wgu, wd):
    per = xe.shape[1]
    rows_in = xe.reshape(-1, D)
    rows_dy = ye.reshape(-1, D)
    hidden, d_pre = expert_pass(rows_in, rows_dy, wgu, wd)
    back = jnp.dot(d_pre, wgu.T, preferred_element_type=jnp.float32).astype(jnp.bfloat16)
    total_gu = jnp.zeros((D, 2 * HID_DEV), jnp.float32)
    total_d = jnp.zeros((HID_DEV, D), jnp.float32)
    for index in range(N_DP):
        low = index * per
        part_gu = jnp.dot(rows_in[low:low + per].T, d_pre[low:low + per], preferred_element_type=jnp.float32)
        part_d = jnp.dot(hidden[low:low + per].T, rows_dy[low:low + per], preferred_element_type=jnp.float32)
        part_gu = lax.optimization_barrier(part_gu.astype(jnp.bfloat16))
        part_d = lax.optimization_barrier(part_d.astype(jnp.bfloat16))
        total_gu = total_gu + part_gu.astype(jnp.float32)
        total_d = total_d + part_d.astype(jnp.float32)
    return (total_gu.astype(jnp.bfloat16), total_d.astype(jnp.bfloat16), back)

def reference(latent, dout, routes, gate_w, norm_gain, w_gate_up, w_down):
    values = latent.astype(jnp.float32)
    inverse = lax.rsqrt(lax.optimization_barrier(jnp.mean(values * values, axis=1, keepdims=True)) + EPS)
    scaled = values * inverse
    expert_in = (scaled * norm_gain[None, :]).astype(jnp.bfloat16)
    inside = routes < E_FL
    chosen = lax.optimization_barrier(jnp.sum(jnp.where(inside, routes, 0), axis=1)).astype(jnp.int32)
    present = jnp.any(inside, axis=1)
    weight = lax.optimization_barrier(jnp.sum(jnp.where(inside, gate_w, jnp.float32(0.0)), axis=1))
    grad_scale = (weight[:, None] * dout.astype(jnp.float32)).astype(jnp.bfloat16)
    blocks = N_DP * N_EXPERT
    onehot = ((chosen[:, None] == jnp.arange(E_FL, dtype=jnp.int32)[None, :]) & present[:, None]).astype(jnp.int32)
    ranks = jnp.cumsum(onehot.reshape(blocks, P_DEV, E_FL), axis=1) - 1
    slot = lax.optimization_barrier(jnp.sum(ranks * onehot.reshape(blocks, P_DEV, E_FL), axis=2)).reshape(-1).astype(jnp.int32)
    target = jnp.where(present, chosen * CAP + slot, E_FL * CAP).astype(jnp.int32)
    block_id = (jnp.arange(TOKENS, dtype=jnp.int32) // P_DEV).astype(jnp.int32)
    empty = jnp.zeros((blocks, E_FL * CAP + 1, D), jnp.bfloat16)
    buf_in = empty.at[block_id, target].set(expert_in)[:, :E_FL * CAP]
    buf_dy = empty.at[block_id, target].set(grad_scale)[:, :E_FL * CAP]

    def arrange(buf):
        shaped = buf.reshape(N_DP, N_EXPERT, E_FL, CAP, D).transpose(2, 0, 1, 3, 4)
        return shaped.reshape(E_FL, N_DP, N_EXPERT * CAP, D)
    arr_in = arrange(buf_in)
    arr_dy = arrange(buf_dy)
    grads_gu = []
    grads_d = []
    tables = []
    for expert in range(E_FL):
        xe = arr_in[expert]
        ye = arr_dy[expert]

        def run(weights):
            return group_work(xe, ye, weights[0], weights[1])
        lo = expert * SLICES
        out_gu, out_d, backs = lax.map(run, (w_gate_up[lo:lo + SLICES], w_down[lo:lo + SLICES]))
        grads_gu.append(out_gu)
        grads_d.append(out_d)
        summed = lax.optimization_barrier(jnp.sum(backs.astype(jnp.float32), axis=0)).astype(jnp.bfloat16)
        tables.append(summed.reshape(N_DP, N_EXPERT, CAP, D))
    table = jnp.stack(tables).transpose(1, 2, 0, 3, 4).reshape(blocks, E_FL * CAP, D)
    table = jnp.concatenate([table, jnp.zeros((blocks, 1, D), jnp.bfloat16)], axis=1)
    d_in = table[block_id, target]
    grad_in = d_in.astype(jnp.float32) * norm_gain[None, :]
    d_latent = inverse * (grad_in - scaled * lax.optimization_barrier(jnp.mean(grad_in * scaled, axis=1, keepdims=True)))
    return (d_latent.astype(jnp.bfloat16), jnp.concatenate(grads_gu, axis=0), jnp.concatenate(grads_d, axis=0))
```

```python
import jax
import jax.numpy as jnp
from jax import lax
from jax.sharding import Mesh, PartitionSpec as P

SLICES = 8
CAP = 4
EPS = 1e-06
Y, C, Z, X = 4, 2, 16, 4
GROUPS = 8
HID = 128
F32 = jnp.float32
BF16 = jnp.bfloat16

SWAP = [
    (c * Z + 2 * e + p, p * Z + 2 * e + c) for c in range(C) for e in range(GROUPS) for p in range(2)
]
FLIP = [(i, i ^ 1) for i in range(Z)]
PLUS = [(i, (i + 1) % X) for i in range(X)]
MINUS = [(i, (i - 1) % X) for i in range(X)]


def outward(rows):
    cut = rows.reshape(GROUPS, CAP, Y, 2, 512)
    return cut.transpose(0, 3, 1, 2, 4).reshape(Z, CAP, 2048)


def homeward(blocks):
    cut = blocks.reshape(GROUPS, 2, CAP, Y, 512)
    return cut.transpose(0, 2, 3, 1, 4).reshape(GROUPS * CAP, 4096)


def gather_x(own):
    half = own.shape[0] // 2
    left = lax.ppermute(own, "x", PLUS)
    right = lax.ppermute(own, "x", MINUS)
    far_a = lax.ppermute(left[:half], "x", PLUS)
    far_b = lax.ppermute(right[half:], "x", MINUS)
    return jnp.concatenate([own, left, right, far_a, far_b], axis=0)


def scatter_x(part):
    n = part.shape[0] // 4
    half = n // 2
    own, left, right = part[:n], part[n : 2 * n], part[2 * n : 3 * n]
    far = part[3 * n :].astype(BF16)
    got_a = lax.ppermute(far[:half], "x", MINUS).astype(F32)
    got_b = lax.ppermute(far[half:], "x", PLUS).astype(F32)
    left = jnp.concatenate([left[:half] + got_a, left[half:]], axis=0).astype(BF16)
    right = jnp.concatenate([right[:half], right[half:] + got_b], axis=0).astype(BF16)
    from_right = lax.ppermute(left, "x", MINUS)
    from_left = lax.ppermute(right, "x", PLUS)
    return own + from_right.astype(F32) + from_left.astype(F32)


def body(latent, dout, routes, gate_w, norm_gain, w_gate_up, w_down):
    zp = lax.axis_index("z") % 2
    even = zp == 0

    piece = jnp.concatenate([w_gate_up[0], w_down[0].T], axis=1)
    piece = lax.ppermute(piece, ("c", "z"), SWAP)
    weights = lax.all_gather(piece, ("c", "y"), axis=0, tiled=True)
    weights = weights.reshape(2, 2048, 3 * HID)

    values = latent.astype(F32)
    inverse = lax.rsqrt(jnp.mean(values * values, axis=1, keepdims=True) + EPS)
    scaled = values * inverse
    expert_in = (scaled * norm_gain[None, :]).astype(BF16)
    inside = routes < GROUPS
    chosen = jnp.sum(jnp.where(inside, routes, 0), axis=1)
    present = jnp.any(inside, axis=1)
    weight = jnp.sum(jnp.where(inside, gate_w, F32(0.0)), axis=1)
    grad_scale = (weight[:, None] * dout.astype(F32)).astype(BF16)
    onehot = (
        (chosen[:, None] == jnp.arange(GROUPS, dtype=jnp.int32)[None, :]) & present[:, None]
    ).astype(jnp.int32)
    slot = jnp.sum((jnp.cumsum(onehot, axis=0) - 1) * onehot, axis=1)
    target = chosen * CAP + slot
    select = (
        (target[None, :] == jnp.arange(GROUPS * CAP, dtype=jnp.int32)[:, None]) & present[None, :]
    ).astype(BF16)
    send_in = jnp.dot(select, expert_in, preferred_element_type=F32).astype(BF16)
    send_dy = jnp.dot(select, grad_scale, preferred_element_type=F32).astype(BF16)

    got_in = lax.all_to_all(outward(send_in), "z", 0, 0, tiled=True).reshape(-1, 2048)
    got_dy = lax.all_to_all(outward(send_dy), "z", 0, 0, tiled=True).reshape(-1, 2048)
    rows_in = gather_x(got_in)
    rows_dy = gather_x(got_dy)

    def joined(rows, low, high):
        part = [
            jnp.dot(rows, weights[g, :, low:high], preferred_element_type=F32) for g in range(2)
        ]
        mine = jnp.where(even, part[0], part[1])
        other = jnp.where(even, part[1], part[0]).astype(BF16)
        return mine + lax.ppermute(other, "z", FLIP).astype(F32)

    pre = joined(rows_in, 0, 2 * HID)
    dh = joined(rows_dy, 2 * HID, 3 * HID)
    gate = pre[:, :HID]
    up = pre[:, HID:]
    sig = jax.nn.sigmoid(gate)
    act = gate * sig
    hidden = act * up
    d_up = dh * act
    d_gate = dh * up * sig * (1.0 + gate * (1.0 - sig))
    mine = jnp.concatenate([d_gate, d_up, hidden], axis=1).astype(BF16)
    other = lax.ppermute(mine, "z", FLIP)
    inner = [jnp.where(even, mine, other), jnp.where(even, other, mine)]

    part_in = sum(
        lax.dot_general(
            inner[g][:, : 2 * HID],
            weights[g, :, : 2 * HID],
            (((1,), (1,)), ((), ())),
            preferred_element_type=F32,
        )
        for g in range(2)
    )
    summed = scatter_x(part_in).astype(BF16)
    home = lax.all_to_all(summed.reshape(Z, CAP, 2048), "z", 0, 0, tiled=True)

    def over_rows(a, b):
        return lax.dot_general(a, b, (((0,), (0,)), ((), ())), preferred_element_type=F32)

    grads = jnp.concatenate(
        [
            jnp.concatenate(
                [
                    over_rows(rows_in, inner[g][:, : 2 * HID]).astype(BF16),
                    over_rows(rows_dy, inner[g][:, 2 * HID :]).astype(BF16),
                ],
                axis=1,
            )
            for g in range(2)
        ],
        axis=0,
    )
    grads = lax.psum_scatter(grads, ("c", "y"), scatter_dimension=0, tiled=True)
    grads = lax.ppermute(grads, ("c", "z"), SWAP)
    grad_gu = grads[:, : 2 * HID][None]
    grad_d = grads[:, 2 * HID :].T[None]

    d_in = lax.dot_general(
        select, homeward(home), (((0,), (0,)), ((), ())), preferred_element_type=F32
    )
    grad_in = d_in * norm_gain[None, :]
    d_latent = inverse * (grad_in - scaled * jnp.mean(grad_in * scaled, axis=1, keepdims=True))
    return d_latent.astype(BF16), grad_gu, grad_d


def solution(mesh):
    fine = Mesh(mesh.devices.reshape(Y, C, Z, X), ("y", "c", "z", "x"))
    rows = P(("y", "c", "z", "x"), None)
    gate_up = P(("z", "x"), ("y", "c"), None)
    down = P(("z", "x"), None, ("y", "c"))
    return jax.shard_map(
        body,
        mesh=fine,
        in_specs=(rows, rows, rows, rows, P(), gate_up, down),
        out_specs=(rows, gate_up, down),
        check_vma=False,
    )
```

```python
import jax
import jax.numpy as jnp
from jax import lax
from jax.experimental import pallas as pl
from jax.experimental.pallas import tpu as pltpu
from jax.sharding import Mesh, PartitionSpec as P


CAP = 4
EPS = 1e-06
Y, C, Z, X = 4, 2, 16, 4
GROUPS = 8
HID = 128
D = 4096
HALF = D // 2
CUT = 512
ROWS = 2 * Z * X * CAP
F32 = jnp.float32
BF16 = jnp.bfloat16

SWAP = [
    (c * Z + 2 * e + p, p * Z + 2 * e + c) for c in range(C) for e in range(GROUPS) for p in range(2)
]
FLIP = [(i, i ^ 1) for i in range(Z)]
PLUS = [(i, (i + 1) % X) for i in range(X)]
MINUS = [(i, (i - 1) % X) for i in range(X)]
ORDER = (0, 3, 1, 2)


def shape(dims, kind):
    return jax.ShapeDtypeStruct(dims, kind)


def iota(dims, axis):
    return lax.broadcasted_iota(jnp.int32, dims, axis)


def placing(routes):
    n = routes.shape[1]
    inside = routes < GROUPS
    chosen = jnp.sum(jnp.where(inside, routes, 0), axis=0, keepdims=True)
    present = jnp.sum(inside.astype(jnp.int32), axis=0, keepdims=True) > 0
    onehot = jnp.where((iota((GROUPS, n), 0) == chosen) & present, 1.0, 0.0)
    earlier = jnp.where(iota((n, n), 0) < iota((n, n), 1), 1.0, 0.0)
    rank = jnp.dot(onehot.astype(BF16), earlier.astype(BF16), preferred_element_type=F32)
    slot = jnp.sum(rank * onehot, axis=0, keepdims=True).astype(jnp.int32)
    return jnp.where(present, chosen * CAP + slot, -1)


def send_kernel(routes, gate_w, latent, dout, gain, out, held):
    n = routes.shape[1]
    where_to = placing(routes[...])
    weight = jnp.sum(
        jnp.where(routes[...] < GROUPS, gate_w[...], F32(0.0)), axis=0, keepdims=True
    )
    row = iota((2 * GROUPS * CAP, n), 0)
    hit = (row // 8 * CAP + row % CAP) == where_to
    take_in = hit & (row % 8 < CAP)
    take_dy = hit & (row % 8 >= CAP)
    factor = jnp.sum(jnp.where(take_dy, weight, F32(0.0)), axis=1, keepdims=True)
    take_in = jnp.where(take_in, 1.0, 0.0).astype(BF16)
    take_dy = jnp.where(take_dy, 1.0, 0.0).astype(BF16)
    square = jnp.zeros((2 * GROUPS * CAP, 1), F32)
    for d in range(D // CUT):
        cols = pl.ds(d * CUT, CUT)
        x = jnp.dot(take_in, latent[:, cols], preferred_element_type=F32)
        held[:, cols] = x
        square = square + jnp.sum(x * x, axis=1, keepdims=True)
    inverse = lax.rsqrt(square * (1.0 / D) + EPS)
    for d in range(D // CUT):
        cols = pl.ds(d * CUT, CUT)
        y = jnp.dot(take_dy, dout[:, cols], preferred_element_type=F32)
        value = held[:, cols] * inverse * gain[:, cols] + y * factor
        for e in range(GROUPS):
            out[2 * e + d % 2, :, pl.ds(d // 2 * CUT, CUT)] = value[8 * e : 8 * e + 8].astype(BF16)


def send_rows(routes, gate_w, latent, dout, gain):
    return pl.pallas_call(
        send_kernel,
        out_shape=shape((Z, 8, HALF), BF16),
        scratch_shapes=[pltpu.VMEM((2 * GROUPS * CAP, D), F32)],
        name="send_rows",
    )(routes, gate_w, latent, dout, gain)


def home_kernel(routes, latent, gain, home, out, grad):
    n = routes.shape[1]
    where_to = placing(routes[...])
    take = jnp.where(iota((GROUPS * CAP, n), 0) == where_to, 1.0, 0.0).astype(BF16)
    for z in range(Z):
        for y in range(Y):
            cols = pl.ds((2 * y + z % 2) * CUT, CUT)
            grad[pl.ds(z // 2 * CAP, CAP), cols] = home[z, :, pl.ds(y * CUT, CUT)].astype(F32)
    x = jnp.dot(take, latent[...], preferred_element_type=F32)
    inverse = lax.rsqrt(jnp.sum(x * x, axis=1, keepdims=True) * (1.0 / D) + EPS)
    scaled = x * inverse
    g = grad[...] * gain[...]
    mean = jnp.sum(g * scaled, axis=1, keepdims=True) * (1.0 / D)
    value = (inverse * (g - scaled * mean)).astype(BF16)
    out[...] = lax.dot_general(
        take, value, (((0,), (0,)), ((), ())), preferred_element_type=F32
    ).astype(BF16)


def home_rows(routes, latent, gain, home):
    return pl.pallas_call(
        home_kernel,
        out_shape=shape(latent.shape, BF16),
        scratch_shapes=[pltpu.VMEM((GROUPS * CAP, D), F32)],
        name="home_rows",
    )(routes, latent, gain, home)


def split_rows(both):
    n = both.shape[1]
    turns = both.reshape(ROWS // 16, 2, 8, n)
    first = turns[:, 0].reshape(ROWS // 2, n)
    second = turns[:, 1].reshape(ROWS // 2, n)
    low = iota((ROWS // 2, n), 0) % 8 < 4
    return first, second, low


def turned(value):
    n = value.shape[1]
    tiles = value.reshape(-1, 8, n)
    return pltpu.roll(tiles, 4, 1).reshape(-1, n)


def mix_kernel(place, own, left, right, far_a, far_b, weights, mine, other, total):
    step = pl.program_id(0)
    rows = jnp.concatenate([own[...], left[...], right[...], far_a[...], far_b[...]], axis=0)
    for g in range(2):
        part = jnp.dot(rows, weights[g], preferred_element_type=F32)

        @pl.when(step == 0)
        def _():
            total[g] = part

        @pl.when(step > 0)
        def _():
            total[g] = total[g] + part

    def packed(both):
        first, second, low = split_rows(both)
        pre = jnp.where(
            low[:, : 2 * HID], first[:, : 2 * HID], turned(second[:, : 2 * HID])
        )
        dh = jnp.where(low[:, :HID], turned(first[:, 2 * HID :]), second[:, 2 * HID :])
        return pre, dh

    @pl.when(step == pl.num_programs(0) - 1)
    def _():
        p = place[0]
        pre, dh = packed(total[p])
        mine[:, : 2 * HID] = pre
        mine[:, 2 * HID :] = dh
        pre, dh = packed(total[1 - p])
        other[:, : 2 * HID] = pre.astype(BF16)
        other[:, 2 * HID :] = dh.astype(BF16)


def row_specs():
    return [
        pl.BlockSpec((n, CUT), lambda i, *_: (0, i))
        for n in (ROWS // 4, ROWS // 4, ROWS // 4, ROWS // 8, ROWS // 8)
    ]


def weight_spec():
    return pl.BlockSpec((2, CUT, 3 * HID), lambda i, *_: (0, i, 0))


def whole(dims):
    return pl.BlockSpec(dims, lambda i, *_: (0,) * len(dims))


def mix(place, blocks, weights):
    dims = (ROWS // 2, 3 * HID)
    return pl.pallas_call(
        mix_kernel,
        grid_spec=pltpu.PrefetchScalarGridSpec(
            num_scalar_prefetch=1,
            grid=(HALF // CUT,),
            in_specs=[*row_specs(), weight_spec()],
            out_specs=[whole(dims), whole(dims)],
            scratch_shapes=[pltpu.VMEM((2, ROWS, 3 * HID), F32)],
        ),
        out_shape=[shape(dims, F32), shape(dims, BF16)],
        name="mix",
    )(place, *blocks, weights)


def gates_kernel(mine, got, out):
    total = mine[...] + got[...].astype(F32)
    gate = total[:, :HID]
    up = total[:, HID : 2 * HID]
    dh = total[:, 2 * HID :]
    sig = jax.nn.sigmoid(gate)
    act = gate * sig
    out[:, :HID] = (dh * up * sig * (1.0 + gate * (1.0 - sig))).astype(BF16)
    out[:, HID : 2 * HID] = (dh * act).astype(BF16)
    out[:, 2 * HID :] = (act * up).astype(BF16)


def gates(mine, got):
    return pl.pallas_call(
        gates_kernel, out_shape=shape(mine.shape, BF16), name="gates"
    )(mine, got)


def back_kernel(place, mine, other, weights, out, inner):
    @pl.when(pl.program_id(0) == 0)
    def _():
        inner[place[0]] = mine[...]
        inner[1 - place[0]] = other[...]

    total = sum(
        lax.dot_general(
            inner[g, :, : 2 * HID],
            weights[g, :, : 2 * HID],
            (((1,), (1,)), ((), ())),
            preferred_element_type=F32,
        )
        for g in range(2)
    ).astype(BF16)
    n = ROWS // 8
    for k, off in enumerate(ORDER):
        out[lax.rem(place[1] + off, X)] = total[n * k : n * k + n]


def back(place, mine, other, weights):
    dims = (ROWS // 2, 3 * HID)
    return pl.pallas_call(
        back_kernel,
        grid_spec=pltpu.PrefetchScalarGridSpec(
            num_scalar_prefetch=1,
            grid=(HALF // CUT,),
            in_specs=[whole(dims), whole(dims), weight_spec()],
            out_specs=pl.BlockSpec((X, ROWS // 8, CUT), lambda i, *_: (0, 0, i)),
            scratch_shapes=[pltpu.VMEM((2, *dims), BF16)],
        ),
        out_shape=shape((X, ROWS // 8, HALF), BF16),
        name="back",
    )(place, mine, other, weights)


def grads_kernel(place, mine, other, own, left, right, far_a, far_b, out, inner):
    @pl.when(pl.program_id(0) == 0)
    def _():
        def spread(value, g):
            value = value.astype(F32)
            n = ROWS // 2
            low = iota((n, 2 * HID), 0) % 8 < 4
            pre = value[:, : 2 * HID]
            hid = value[:, 2 * HID :]
            zero = F32(0.0)
            first = jnp.where(low, pre, zero), jnp.where(low[:, :HID], zero, turned(hid))
            second = jnp.where(low, turned(pre), zero), jnp.where(low[:, :HID], zero, hid)
            for k, cols in ((0, pl.ds(0, 2 * HID)), (1, pl.ds(2 * HID, HID))):
                width = first[k].shape[1]
                pair = jnp.stack(
                    [first[k].reshape(-1, 8, width), second[k].reshape(-1, 8, width)], axis=1
                )
                inner[g, :, cols] = pair.reshape(ROWS, width).astype(BF16)

        spread(mine[...], place[0])
        spread(other[...], 1 - place[0])

    rows = jnp.concatenate([own[...], left[...], right[...], far_a[...], far_b[...]], axis=0)
    for g in range(2):
        out[g, 0] = lax.dot_general(
            rows, inner[g], (((0,), (0,)), ((), ())), preferred_element_type=F32
        ).astype(BF16)


def grads(place, mine, other, blocks):
    dims = (ROWS // 2, 3 * HID)
    return pl.pallas_call(
        grads_kernel,
        grid_spec=pltpu.PrefetchScalarGridSpec(
            num_scalar_prefetch=1,
            grid=(HALF // CUT,),
            in_specs=[whole(dims), whole(dims), *row_specs()],
            out_specs=pl.BlockSpec((2, 1, CUT, 3 * HID), lambda i, *_: (0, i, 0, 0)),
            scratch_shapes=[pltpu.VMEM((2, ROWS, 3 * HID), BF16)],
        ),
        out_shape=shape((2, HALF // CUT, CUT, 3 * HID), BF16),
        name="grads",
    )(place, mine, other, *blocks)


def gather_x(own):
    half = own.shape[0] // 2
    left = lax.ppermute(own, "x", PLUS)
    right = lax.ppermute(own, "x", MINUS)
    far_a = lax.ppermute(left[:half], "x", PLUS)
    far_b = lax.ppermute(right[half:], "x", MINUS)
    return own, left, right, far_a, far_b


def work(latent, dout, routes, gate_w, norm_gain, w_gate_up, w_down):
    place = jnp.stack([lax.axis_index("z") % 2, lax.axis_index("x")]).astype(jnp.int32)
    gain = norm_gain[None, :]
    routes = routes.T

    send = send_rows(routes, gate_w.T, latent, dout, gain)
    piece = jnp.concatenate([w_gate_up[0], w_down[0].T], axis=1)
    got = lax.all_to_all(send, "z", 0, 0, tiled=True)
    piece = lax.ppermute(piece, ("c", "z"), SWAP)
    weights = lax.all_gather(piece, ("c", "y"), axis=0, tiled=True)
    weights = weights.reshape(2, HALF, 3 * HID)

    blocks = gather_x(got.reshape(ROWS // 4, HALF))
    mine, other = mix(place, blocks, weights)
    inner = gates(mine, lax.ppermute(other, "z", FLIP))
    outer = lax.ppermute(inner, "z", FLIP)

    grad = grads(place, inner, outer, blocks).reshape(2 * HALF, 3 * HID)
    grad = lax.psum_scatter(grad, ("c", "y"), scatter_dimension=0, tiled=True)
    grad = lax.ppermute(grad, ("c", "z"), SWAP)
    grad_gu = grad[:, : 2 * HID][None]
    grad_d = grad[:, 2 * HID :].T[None]

    part = lax.all_to_all(back(place, inner, outer, weights), "x", 0, 0, tiled=True)
    summed = jnp.sum(part.astype(F32), axis=0).astype(BF16)
    home = lax.all_to_all(summed.reshape(Z, CAP, HALF), "z", 0, 0, tiled=True)
    return home_rows(routes, latent, gain, home), grad_gu, grad_d


def solution(mesh):
    fine = Mesh(mesh.devices.reshape(Y, C, Z, X), ("y", "c", "z", "x"))
    rows = P(("y", "c", "z", "x"), None)
    gate_up = P(("z", "x"), ("y", "c"), None)
    down = P(("z", "x"), None, ("y", "c"))
    return jax.shard_map(
        work,
        mesh=fine,
        in_specs=(rows, rows, rows, rows, P(), gate_up, down),
        out_specs=(rows, gate_up, down),
        check_vma=False,
    )
```

```python
import functools

import jax
import jax.numpy as jnp
from jax import lax
from jax.experimental import pallas as pl
from jax.experimental.pallas import tpu as pltpu
from jax.sharding import Mesh, PartitionSpec as P


CAP = 4
EPS = 1e-06
Y, C, Z, X = 4, 2, 16, 4
GROUPS = 8
HID = 128
D = 4096
HALF = D // 2
CUT = 512
ROWS = 2 * Z * X * CAP
F32 = jnp.float32
BF16 = jnp.bfloat16

SWAP = [
    (c * Z + 2 * e + p, p * Z + 2 * e + c) for c in range(C) for e in range(GROUPS) for p in range(2)
]
FLIP = [(i, i ^ 1) for i in range(Z)]
PLUS = [(i, (i + 1) % X) for i in range(X)]
MINUS = [(i, (i - 1) % X) for i in range(X)]
ORDER = (0, 3, 1, 2)


def shape(dims, kind):
    return jax.ShapeDtypeStruct(dims, kind)


def iota(dims, axis):
    return lax.broadcasted_iota(jnp.int32, dims, axis)


def placing(routes):
    n = routes.shape[1]
    inside = routes < GROUPS
    chosen = jnp.sum(jnp.where(inside, routes, 0), axis=0, keepdims=True)
    present = jnp.sum(inside.astype(jnp.int32), axis=0, keepdims=True) > 0
    onehot = jnp.where((iota((GROUPS, n), 0) == chosen) & present, 1.0, 0.0)
    earlier = jnp.where(iota((n, n), 0) < iota((n, n), 1), 1.0, 0.0)
    rank = jnp.dot(onehot.astype(BF16), earlier.astype(BF16), preferred_element_type=F32)
    slot = jnp.sum(rank * onehot, axis=0, keepdims=True).astype(jnp.int32)
    return jnp.where(present, chosen * CAP + slot, -1)


def send_kernel(routes, gate_w, latent, dout, gain, gate_up, down, out, piece, held):
    piece[:, : 2 * HID] = gate_up[0]
    piece[:, 2 * HID :] = down[0].astype(F32).T.astype(BF16)
    n = routes.shape[1]
    where_to = placing(routes[...])
    weight = jnp.sum(
        jnp.where(routes[...] < GROUPS, gate_w[...], F32(0.0)), axis=0, keepdims=True
    )
    row = iota((2 * GROUPS * CAP, n), 0)
    hit = (row // 8 * CAP + row % CAP) == where_to
    take_in = hit & (row % 8 < CAP)
    take_dy = hit & (row % 8 >= CAP)
    factor = jnp.sum(jnp.where(take_dy, weight, F32(0.0)), axis=1, keepdims=True)
    take_in = jnp.where(take_in, 1.0, 0.0).astype(BF16)
    take_dy = jnp.where(take_dy, 1.0, 0.0).astype(BF16)
    square = jnp.zeros((2 * GROUPS * CAP, 1), F32)
    for d in range(D // CUT):
        cols = pl.ds(d * CUT, CUT)
        x = jnp.dot(take_in, latent[:, cols], preferred_element_type=F32)
        held[:, cols] = x
        square = square + jnp.sum(x * x, axis=1, keepdims=True)
    inverse = lax.rsqrt(square * (1.0 / D) + EPS)
    for d in range(D // CUT):
        cols = pl.ds(d * CUT, CUT)
        y = jnp.dot(take_dy, dout[:, cols], preferred_element_type=F32)
        value = held[:, cols] * inverse * gain[:, cols] + y * factor
        for e in range(GROUPS):
            out[2 * e + d % 2, :, pl.ds(d // 2 * CUT, CUT)] = value[8 * e : 8 * e + 8].astype(BF16)


def send_rows(*args):
    return pl.pallas_call(
        send_kernel,
        out_shape=[shape((Z, 8, HALF), BF16), shape((CUT, 3 * HID), BF16)],
        scratch_shapes=[pltpu.VMEM((2 * GROUPS * CAP, D), F32)],
        name="send_rows",
    )(*args)


def hold_kernel(piece, out):
    out[...] = piece[...]


def hold(piece):
    return pl.pallas_call(hold_kernel, out_shape=shape(piece.shape, BF16), name="hold")(piece)


def home_kernel(routes, latent, gain, home, out, grad):
    n = routes.shape[1]
    where_to = placing(routes[...])
    take = jnp.where(iota((GROUPS * CAP, n), 0) == where_to, 1.0, 0.0).astype(BF16)
    for z in range(Z):
        for y in range(Y):
            cols = pl.ds((2 * y + z % 2) * CUT, CUT)
            grad[pl.ds(z // 2 * CAP, CAP), cols] = home[z, :, pl.ds(y * CUT, CUT)].astype(F32)
    x = jnp.dot(take, latent[...], preferred_element_type=F32)
    inverse = lax.rsqrt(jnp.sum(x * x, axis=1, keepdims=True) * (1.0 / D) + EPS)
    scaled = x * inverse
    g = grad[...] * gain[...]
    mean = jnp.sum(g * scaled, axis=1, keepdims=True) * (1.0 / D)
    value = (inverse * (g - scaled * mean)).astype(BF16)
    out[...] = lax.dot_general(
        take, value, (((0,), (0,)), ((), ())), preferred_element_type=F32
    ).astype(BF16)


def home_rows(routes, latent, gain, home):
    return pl.pallas_call(
        home_kernel,
        out_shape=shape(latent.shape, BF16),
        scratch_shapes=[pltpu.VMEM((GROUPS * CAP, D), F32)],
        name="home_rows",
    )(routes, latent, gain, home)


def turned(value):
    n = value.shape[1]
    tiles = value.reshape(-1, 8, n)
    return pltpu.roll(tiles, 4, 1).reshape(-1, n)


def mix_kernel(count, place, *refs):
    blocks, weights = refs[:count], refs[count]
    mine, other, total = refs[-3:]
    step = pl.program_id(0)
    rows = blocks[0][...]
    if count > 1:
        rows = jnp.concatenate([block[...] for block in blocks], axis=0)
    for g in range(2):
        part = jnp.dot(rows, weights[g], preferred_element_type=F32)

        @pl.when(step == 0)
        def _():
            total[g] = part

        @pl.when(step > 0)
        def _():
            total[g] = total[g] + part

    def packed(both):
        turns = both.reshape(-1, 2, 8, 3 * HID)
        first = turns[:, 0].reshape(-1, 3 * HID)
        second = turns[:, 1].reshape(-1, 3 * HID)
        low = iota((first.shape[0], 2 * HID), 0) % 8 < 4
        pre = jnp.where(low, first[:, : 2 * HID], turned(second[:, : 2 * HID]))
        dh = jnp.where(low[:, :HID], turned(first[:, 2 * HID :]), second[:, 2 * HID :])
        return pre, dh

    @pl.when(step == pl.num_programs(0) - 1)
    def _():
        pre, dh = packed(total[place[0]])
        mine[:, : 2 * HID] = pre
        mine[:, 2 * HID :] = dh
        pre, dh = packed(total[1 - place[0]])
        other[:, : 2 * HID] = pre.astype(BF16)
        other[:, 2 * HID :] = dh.astype(BF16)


def row_specs():
    return [
        pl.BlockSpec((n, CUT), lambda i, *_: (0, i))
        for n in (ROWS // 4, ROWS // 4, ROWS // 4, ROWS // 8, ROWS // 8)
    ]


def weight_spec():
    return pl.BlockSpec((2, CUT, 3 * HID), lambda i, *_: (0, i, 0))


def whole(dims):
    return pl.BlockSpec(dims, lambda i, *_: (0,) * len(dims))


def mix(place, at, blocks, weights, so_far):
    rows = sum(block.shape[0] for block in blocks)
    part = pl.BlockSpec((rows // 2, 3 * HID), lambda i, *_: (at, 0))
    dims = (ROWS // 2, 3 * HID)
    hold = [pl.BlockSpec(memory_space=pl.ANY)] * len(so_far)
    first = 2 + len(blocks)
    return pl.pallas_call(
        functools.partial(mix_kernel, len(blocks)),
        grid_spec=pltpu.PrefetchScalarGridSpec(
            num_scalar_prefetch=1,
            grid=(HALF // CUT,),
            in_specs=[
                *[pl.BlockSpec((b.shape[0], CUT), lambda i, *_: (0, i)) for b in blocks],
                weight_spec(),
                *hold,
            ],
            out_specs=[part, part],
            scratch_shapes=[pltpu.VMEM((2, rows, 3 * HID), F32)],
        ),
        out_shape=[shape(dims, F32), shape(dims, BF16)],
        input_output_aliases={first + k: k for k in range(len(so_far))},
    )(place, *blocks, weights, *so_far)


def gates_kernel(mine, got, out):
    total = mine[...] + got[...].astype(F32)
    gate = total[:, :HID]
    up = total[:, HID : 2 * HID]
    dh = total[:, 2 * HID :]
    sig = jax.nn.sigmoid(gate)
    act = gate * sig
    out[:, :HID] = (dh * up * sig * (1.0 + gate * (1.0 - sig))).astype(BF16)
    out[:, HID : 2 * HID] = (dh * act).astype(BF16)
    out[:, 2 * HID :] = (act * up).astype(BF16)


def gates(mine, got):
    return pl.pallas_call(
        gates_kernel, out_shape=shape(mine.shape, BF16), name="gates"
    )(mine, got)


def back_kernel(place, mine, other, weights, out, inner):
    @pl.when(pl.program_id(0) == 0)
    def _():
        inner[place[0]] = mine[...]
        inner[1 - place[0]] = other[...]

    total = sum(
        lax.dot_general(
            inner[g, :, : 2 * HID],
            weights[g, :, : 2 * HID],
            (((1,), (1,)), ((), ())),
            preferred_element_type=F32,
        )
        for g in range(2)
    ).astype(BF16)
    n = ROWS // 8
    for k, off in enumerate(ORDER):
        out[lax.rem(place[1] + off, X)] = total[n * k : n * k + n]


def back(place, mine, other, weights):
    dims = (ROWS // 2, 3 * HID)
    return pl.pallas_call(
        back_kernel,
        grid_spec=pltpu.PrefetchScalarGridSpec(
            num_scalar_prefetch=1,
            grid=(HALF // CUT,),
            in_specs=[whole(dims), whole(dims), weight_spec()],
            out_specs=pl.BlockSpec((X, ROWS // 8, CUT), lambda i, *_: (0, 0, i)),
            scratch_shapes=[pltpu.VMEM((2, *dims), BF16)],
        ),
        out_shape=shape((X, ROWS // 8, HALF), BF16),
        name="back",
    )(place, mine, other, weights)


def grads_kernel(place, value, own, left, right, far_a, far_b, *refs):
    out, inner = refs[-2:]

    @pl.when(pl.program_id(0) == 0)
    def _():
        both = value[...].astype(F32)
        low = iota((ROWS // 2, 2 * HID), 0) % 8 < 4
        pre = both[:, : 2 * HID]
        hid = both[:, 2 * HID :]
        zero = F32(0.0)
        first = jnp.where(low, pre, zero), jnp.where(low[:, :HID], zero, turned(hid))
        second = jnp.where(low, turned(pre), zero), jnp.where(low[:, :HID], zero, hid)
        for k, cols in ((0, pl.ds(0, 2 * HID)), (1, pl.ds(2 * HID, HID))):
            width = first[k].shape[1]
            pair = jnp.stack(
                [first[k].reshape(-1, 8, width), second[k].reshape(-1, 8, width)], axis=1
            )
            inner[:, cols] = pair.reshape(ROWS, width).astype(BF16)

    rows = jnp.concatenate([own[...], left[...], right[...], far_a[...], far_b[...]], axis=0)
    out[0, 0] = lax.dot_general(
        rows, inner[...], (((0,), (0,)), ((), ())), preferred_element_type=F32
    ).astype(BF16)


def grads(place, turn, value, blocks, so_far):
    hold = [pl.BlockSpec(memory_space=pl.ANY)] * len(so_far)

    def at(i, place):
        slot = place[2]
        return (slot if turn == 0 else 1 - slot), i, 0, 0

    return pl.pallas_call(
        grads_kernel,
        grid_spec=pltpu.PrefetchScalarGridSpec(
            num_scalar_prefetch=1,
            grid=(HALF // CUT,),
            in_specs=[whole((ROWS // 2, 3 * HID)), *row_specs(), *hold],
            out_specs=pl.BlockSpec((1, 1, CUT, 3 * HID), at),
            scratch_shapes=[pltpu.VMEM((ROWS, 3 * HID), BF16)],
        ),
        out_shape=shape((2, HALF // CUT, CUT, 3 * HID), BF16),
        input_output_aliases={2 + len(blocks): 0} if so_far else {},
    )(place, value, *blocks, *so_far)


def work(latent, dout, routes, gate_w, norm_gain, w_gate_up, w_down):
    zp = lax.axis_index("z") % 2
    core = lax.axis_index("c")
    place = jnp.stack([zp, lax.axis_index("x"), (zp + core) % 2]).astype(jnp.int32)
    gain = norm_gain[None, :]
    routes = routes.T

    send, piece = send_rows(routes, gate_w.T, latent, dout, gain, w_gate_up, w_down)
    piece = lax.ppermute(piece, ("c", "z"), SWAP)
    got = lax.all_to_all(send, "z", 0, 0, tiled=True)
    weights = lax.all_gather(hold(piece), ("c", "y"), axis=0, tiled=True)
    weights = weights.reshape(2, HALF, 3 * HID)

    own = got.reshape(ROWS // 4, HALF)
    half = own.shape[0] // 2
    left = lax.ppermute(own, "x", PLUS)
    right = lax.ppermute(own, "x", MINUS)
    far_a = lax.ppermute(left[:half], "x", PLUS)
    far_b = lax.ppermute(right[half:], "x", MINUS)
    blocks = own, left, right, far_a, far_b

    parts = ()
    for at, some in enumerate(((own,), (left,), (right,), (far_a, far_b))):
        parts = mix(place, at, some, weights, parts)
    mine, other = parts
    inner = gates(mine, lax.ppermute(other, "z", FLIP))
    outer = lax.ppermute(inner, "z", FLIP)

    grad = grads(place, 0, inner, blocks, ())
    part = back(place, inner, outer, weights)
    part = lax.all_to_all(part, "x", 0, 0, tiled=True)
    grad = grads(place, 1, outer, blocks, (grad,))
    partner = lax.ppermute(grad[1], "c", [(0, 1), (1, 0)])
    grad = (grad[0].astype(F32) + partner.astype(F32)).astype(BF16).reshape(HALF, 3 * HID)
    grad = lax.psum_scatter(grad, "y", scatter_dimension=0, tiled=True)
    grad = lax.ppermute(grad, ("c", "z"), SWAP)
    grad_gu = grad[:, : 2 * HID][None]
    grad_d = grad[:, 2 * HID :].T[None]

    summed = jnp.sum(part.astype(F32), axis=0).astype(BF16)
    home = lax.all_to_all(summed.reshape(Z, CAP, HALF), "z", 0, 0, tiled=True)
    return home_rows(routes, latent, gain, home), grad_gu, grad_d


def solution(mesh):
    fine = Mesh(mesh.devices.reshape(Y, C, Z, X), ("y", "c", "z", "x"))
    rows = P(("y", "c", "z", "x"), None)
    gate_up = P(("z", "x"), ("y", "c"), None)
    down = P(("z", "x"), None, ("y", "c"))
    return jax.shard_map(
        work,
        mesh=fine,
        in_specs=(rows, rows, rows, rows, P(), gate_up, down),
        out_specs=(rows, gate_up, down),
        check_vma=False,
    )
```

```python
import functools

import jax
import jax.numpy as jnp
from jax import lax
from jax.experimental import pallas as pl
from jax.experimental.pallas import tpu as pltpu
from jax.sharding import Mesh, PartitionSpec as P


CAP = 4
EPS = 1e-06
Y, C, Z, X = 4, 2, 16, 4
GROUPS = 8
HID = 128
D = 4096
HALF = D // 2
CUT = 512
ROWS = 2 * Z * X * CAP
F32 = jnp.float32
BF16 = jnp.bfloat16

SWAP = [
    (c * Z + 2 * e + p, p * Z + 2 * e + c) for c in range(C) for e in range(GROUPS) for p in range(2)
]
FLIP = [(i, i ^ 1) for i in range(Z)]
PLUS = [(i, (i + 1) % X) for i in range(X)]
MINUS = [(i, (i - 1) % X) for i in range(X)]
TURN = [(0, 1), (1, 0)]
ORDER = (0, 3, 1, 2)


def shape(dims, kind):
    return jax.ShapeDtypeStruct(dims, kind)


def iota(dims, axis):
    return lax.broadcasted_iota(jnp.int32, dims, axis)


def placing(routes):
    n = routes.shape[1]
    inside = routes < GROUPS
    chosen = jnp.sum(jnp.where(inside, routes, 0), axis=0, keepdims=True)
    present = jnp.sum(inside.astype(jnp.int32), axis=0, keepdims=True) > 0
    onehot = jnp.where((iota((GROUPS, n), 0) == chosen) & present, 1.0, 0.0)
    earlier = jnp.where(iota((n, n), 0) < iota((n, n), 1), 1.0, 0.0)
    rank = jnp.dot(onehot.astype(BF16), earlier.astype(BF16), preferred_element_type=F32)
    slot = jnp.sum(rank * onehot, axis=0, keepdims=True).astype(jnp.int32)
    return jnp.where(present, chosen * CAP + slot, -1)


def send_kernel(routes, gate_w, latent, dout, gain, gate_up, down, out, piece, held):
    piece[:, : 2 * HID] = gate_up[0]
    piece[:, 2 * HID :] = down[0].astype(F32).T.astype(BF16)
    n = routes.shape[1]
    where_to = placing(routes[...])
    weight = jnp.sum(
        jnp.where(routes[...] < GROUPS, gate_w[...], F32(0.0)), axis=0, keepdims=True
    )
    row = iota((2 * GROUPS * CAP, n), 0)
    hit = (row // 8 * CAP + row % CAP) == where_to
    take_in = hit & (row % 8 < CAP)
    take_dy = hit & (row % 8 >= CAP)
    factor = jnp.sum(jnp.where(take_dy, weight, F32(0.0)), axis=1, keepdims=True)
    take_in = jnp.where(take_in, 1.0, 0.0).astype(BF16)
    take_dy = jnp.where(take_dy, 1.0, 0.0).astype(BF16)
    square = jnp.zeros((2 * GROUPS * CAP, 1), F32)
    for d in range(D // CUT):
        cols = pl.ds(d * CUT, CUT)
        x = jnp.dot(take_in, latent[:, cols], preferred_element_type=F32)
        held[:, cols] = x
        square = square + jnp.sum(x * x, axis=1, keepdims=True)
    inverse = lax.rsqrt(square * (1.0 / D) + EPS)
    for d in range(D // CUT):
        cols = pl.ds(d * CUT, CUT)
        y = jnp.dot(take_dy, dout[:, cols], preferred_element_type=F32)
        value = held[:, cols] * inverse * gain[:, cols] + y * factor
        for e in range(GROUPS):
            out[2 * e + d % 2, :, pl.ds(d // 2 * CUT, CUT)] = value[8 * e : 8 * e + 8].astype(BF16)


def send_rows(*args):
    return pl.pallas_call(
        send_kernel,
        out_shape=[shape((Z, 8, HALF), BF16), shape((CUT, 3 * HID), BF16)],
        scratch_shapes=[pltpu.VMEM((2 * GROUPS * CAP, D), F32)],
        name="send_rows",
    )(*args)


def join_kernel(own, left, right, far_a, far_b, out):
    out[pl.ds(0, CUT), :] = own[...]
    out[pl.ds(CUT, CUT), :] = left[...]
    out[pl.ds(2 * CUT, CUT), :] = right[...]
    out[pl.ds(3 * CUT, CUT // 2), :] = far_a[...]
    out[pl.ds(3 * CUT + CUT // 2, CUT // 2), :] = far_b[...]


def join(*blocks):
    return pl.pallas_call(
        join_kernel, out_shape=shape((HALF, 3 * HID), BF16), name="join"
    )(*blocks)


def home_kernel(routes, latent, gain, home, out, grad):
    n = routes.shape[1]
    where_to = placing(routes[...])
    take = jnp.where(iota((GROUPS * CAP, n), 0) == where_to, 1.0, 0.0).astype(BF16)
    for z in range(Z):
        for y in range(Y):
            cols = pl.ds((2 * y + z % 2) * CUT, CUT)
            grad[pl.ds(z // 2 * CAP, CAP), cols] = home[z, :, pl.ds(y * CUT, CUT)].astype(F32)
    x = jnp.dot(take, latent[...], preferred_element_type=F32)
    inverse = lax.rsqrt(jnp.sum(x * x, axis=1, keepdims=True) * (1.0 / D) + EPS)
    scaled = x * inverse
    g = grad[...] * gain[...]
    mean = jnp.sum(g * scaled, axis=1, keepdims=True) * (1.0 / D)
    value = (inverse * (g - scaled * mean)).astype(BF16)
    out[...] = lax.dot_general(
        take, value, (((0,), (0,)), ((), ())), preferred_element_type=F32
    ).astype(BF16)


def home_rows(routes, latent, gain, home):
    return pl.pallas_call(
        home_kernel,
        out_shape=shape(latent.shape, BF16),
        scratch_shapes=[pltpu.VMEM((GROUPS * CAP, D), F32)],
        name="home_rows",
    )(routes, latent, gain, home)


def turned(value):
    n = value.shape[1]
    tiles = value.reshape(-1, 8, n)
    return pltpu.roll(tiles, 4, 1).reshape(-1, n)


def mix_kernel(count, place, *refs):
    blocks, weights = refs[:count], refs[count : count + 2]
    mine, other, total = refs[-3:]
    step = pl.program_id(0)
    rows = blocks[0][...]
    if count > 1:
        rows = jnp.concatenate([block[...] for block in blocks], axis=0)
    for g in range(2):
        part = jnp.dot(rows, weights[g][...], preferred_element_type=F32)

        @pl.when(step == 0)
        def _():
            total[g] = part

        @pl.when(step > 0)
        def _():
            total[g] = total[g] + part

    def packed(both):
        turns = both.reshape(-1, 2, 8, 3 * HID)
        first = turns[:, 0].reshape(-1, 3 * HID)
        second = turns[:, 1].reshape(-1, 3 * HID)
        low = iota((first.shape[0], 2 * HID), 0) % 8 < 4
        pre = jnp.where(low, first[:, : 2 * HID], turned(second[:, : 2 * HID]))
        dh = jnp.where(low[:, :HID], turned(first[:, 2 * HID :]), second[:, 2 * HID :])
        return pre, dh

    @pl.when(step == pl.num_programs(0) - 1)
    def _():
        pre, dh = packed(total[place[2]])
        mine[:, : 2 * HID] = pre
        mine[:, 2 * HID :] = dh
        pre, dh = packed(total[1 - place[2]])
        other[:, : 2 * HID] = pre.astype(BF16)
        other[:, 2 * HID :] = dh.astype(BF16)


def row_specs():
    return [
        pl.BlockSpec((n, CUT), lambda i, place: (0, place[3 + i]))
        for n in (ROWS // 4, ROWS // 4, ROWS // 4, ROWS // 8, ROWS // 8)
    ]


def weight_specs():
    return [pl.BlockSpec((CUT, 3 * HID), lambda i, *_: (i, 0))] * 2


def whole(dims):
    return pl.BlockSpec(dims, lambda i, *_: (0,) * len(dims))


def mix(place, at, blocks, weights, so_far):
    rows = sum(block.shape[0] for block in blocks)
    part = pl.BlockSpec((rows // 2, 3 * HID), lambda i, *_: (at, 0))
    dims = (ROWS // 2, 3 * HID)
    hold = [pl.BlockSpec(memory_space=pl.ANY)] * len(so_far)
    first = 3 + len(blocks)
    return pl.pallas_call(
        functools.partial(mix_kernel, len(blocks)),
        grid_spec=pltpu.PrefetchScalarGridSpec(
            num_scalar_prefetch=1,
            grid=(HALF // CUT,),
            in_specs=[
                *[
                    pl.BlockSpec((b.shape[0], CUT), lambda i, place: (0, place[3 + i]))
                    for b in blocks
                ],
                *weight_specs(),
                *hold,
            ],
            out_specs=[part, part],
            scratch_shapes=[pltpu.VMEM((2, rows, 3 * HID), F32)],
        ),
        out_shape=[shape(dims, F32), shape(dims, BF16)],
        input_output_aliases={first + k: k for k in range(len(so_far))},
    )(place, *blocks, *weights, *so_far)


def gates_kernel(mine, got, out):
    total = mine[...] + got[...].astype(F32)
    gate = total[:, :HID]
    up = total[:, HID : 2 * HID]
    dh = total[:, 2 * HID :]
    sig = jax.nn.sigmoid(gate)
    act = gate * sig
    out[:, :HID] = (dh * up * sig * (1.0 + gate * (1.0 - sig))).astype(BF16)
    out[:, HID : 2 * HID] = (dh * act).astype(BF16)
    out[:, 2 * HID :] = (act * up).astype(BF16)


def gates(mine, got):
    return pl.pallas_call(
        gates_kernel, out_shape=shape(mine.shape, BF16), name="gates"
    )(mine, got)


def back_kernel(place, mine, other, weights_a, weights_b, out, inner):
    weights = weights_a, weights_b

    @pl.when(pl.program_id(0) == 0)
    def _():
        inner[place[2]] = mine[...]
        inner[1 - place[2]] = other[...]

    total = sum(
        lax.dot_general(
            inner[g, :, : 2 * HID],
            weights[g][:, : 2 * HID],
            (((1,), (1,)), ((), ())),
            preferred_element_type=F32,
        )
        for g in range(2)
    ).astype(BF16)
    n = ROWS // 8
    for k, off in enumerate(ORDER):
        out[lax.rem(place[1] + off, X)] = total[n * k : n * k + n]


def back(place, mine, other, weights):
    dims = (ROWS // 2, 3 * HID)
    return pl.pallas_call(
        back_kernel,
        grid_spec=pltpu.PrefetchScalarGridSpec(
            num_scalar_prefetch=1,
            grid=(HALF // CUT,),
            in_specs=[whole(dims), whole(dims), *weight_specs()],
            out_specs=pl.BlockSpec((X, ROWS // 8, CUT), lambda i, place: (0, 0, place[3 + i])),
            scratch_shapes=[pltpu.VMEM((2, *dims), BF16)],
        ),
        out_shape=shape((X, ROWS // 8, HALF), BF16),
        name="back",
    )(place, mine, other, *weights)


def grads_kernel(place, value, own, left, right, far_a, far_b, *refs):
    out, inner = refs[-2:]

    @pl.when(pl.program_id(0) == 0)
    def _():
        both = value[...].astype(F32)
        low = iota((ROWS // 2, 2 * HID), 0) % 8 < 4
        pre = both[:, : 2 * HID]
        hid = both[:, 2 * HID :]
        zero = F32(0.0)
        first = jnp.where(low, pre, zero), jnp.where(low[:, :HID], zero, turned(hid))
        second = jnp.where(low, turned(pre), zero), jnp.where(low[:, :HID], zero, hid)
        for k, cols in ((0, pl.ds(0, 2 * HID)), (1, pl.ds(2 * HID, HID))):
            width = first[k].shape[1]
            pair = jnp.stack(
                [first[k].reshape(-1, 8, width), second[k].reshape(-1, 8, width)], axis=1
            )
            inner[:, cols] = pair.reshape(ROWS, width).astype(BF16)

    rows = jnp.concatenate([own[...], left[...], right[...], far_a[...], far_b[...]], axis=0)
    out[0, 0] = lax.dot_general(
        rows, inner[...], (((0,), (0,)), ((), ())), preferred_element_type=F32
    ).astype(BF16)


def grads(place, turn, value, blocks, so_far):
    hold = [pl.BlockSpec(memory_space=pl.ANY)] * len(so_far)

    def at(i, place):
        slot = place[2]
        return (slot if turn == 0 else 1 - slot), i, 0, 0

    return pl.pallas_call(
        grads_kernel,
        grid_spec=pltpu.PrefetchScalarGridSpec(
            num_scalar_prefetch=1,
            grid=(HALF // CUT,),
            in_specs=[whole((ROWS // 2, 3 * HID)), *row_specs(), *hold],
            out_specs=pl.BlockSpec((1, 1, CUT, 3 * HID), at),
            scratch_shapes=[pltpu.VMEM((ROWS, 3 * HID), BF16)],
        ),
        out_shape=shape((2, HALF // CUT, CUT, 3 * HID), BF16),
        input_output_aliases={2 + len(blocks): 0} if so_far else {},
    )(place, value, *blocks, *so_far)


def gathered(own, axis):
    half = own.shape[0] // 2
    left = lax.ppermute(own, axis, PLUS)
    right = lax.ppermute(own, axis, MINUS)
    far_a = lax.ppermute(left[:half], axis, PLUS)
    far_b = lax.ppermute(right[half:], axis, MINUS)
    return own, left, right, far_a, far_b


def scattered(parts):
    own, left, right, far = parts
    half = own.shape[0] // 2
    far = far.astype(BF16)
    got_a = lax.ppermute(far[:half], "y", MINUS).astype(F32)
    got_b = lax.ppermute(far[half:], "y", PLUS).astype(F32)
    left = jnp.concatenate([left[:half] + got_a, left[half:]], axis=0).astype(BF16)
    right = jnp.concatenate([right[:half], right[half:] + got_b], axis=0).astype(BF16)
    left = lax.ppermute(left, "y", MINUS)
    right = lax.ppermute(right, "y", PLUS)
    return (own + left.astype(F32) + right.astype(F32)).astype(BF16)


def work(latent, dout, routes, gate_w, norm_gain, w_gate_up, w_down):
    zp = lax.axis_index("z") % 2
    core = lax.axis_index("c")
    y = lax.axis_index("y")
    place = jnp.stack(
        [zp, lax.axis_index("x"), (zp + core) % 2, *[(y + off) % Y for off in ORDER]]
    ).astype(jnp.int32)
    gain = norm_gain[None, :]
    routes = routes.T

    send, piece = send_rows(routes, gate_w.T, latent, dout, gain, w_gate_up, w_down)
    piece = lax.ppermute(piece, ("c", "z"), SWAP)
    got = lax.all_to_all(send, "z", 0, 0, tiled=True)
    mine = join(*gathered(piece, "y"))
    weights = mine, lax.ppermute(mine, "c", TURN)

    blocks = gathered(got.reshape(ROWS // 4, HALF), "x")
    parts = mix(place, 0, blocks[:3], weights, ())
    mine, other = mix(place, 3, blocks[3:], weights, parts)
    inner = gates(mine, lax.ppermute(other, "z", FLIP))
    outer = lax.ppermute(inner, "z", FLIP)

    grad = grads(place, 0, inner, blocks, ())
    part = back(place, inner, outer, weights)
    part = lax.all_to_all(part, "x", 0, 0, tiled=True)
    grad = grads(place, 1, outer, blocks, (grad,))
    partner = lax.ppermute(grad[1], "c", TURN)
    grad = scattered([grad[0, k].astype(F32) + partner[k].astype(F32) for k in range(Y)])
    grad = lax.ppermute(grad, ("c", "z"), SWAP)
    grad_gu = grad[:, : 2 * HID][None]
    grad_d = grad[:, 2 * HID :].T[None]

    summed = jnp.sum(part.astype(F32), axis=0).astype(BF16)
    home = lax.all_to_all(summed.reshape(Z, CAP, HALF), "z", 0, 0, tiled=True)
    return home_rows(routes, latent, gain, home), grad_gu, grad_d


def solution(mesh):
    fine = Mesh(mesh.devices.reshape(Y, C, Z, X), ("y", "c", "z", "x"))
    rows = P(("y", "c", "z", "x"), None)
    gate_up = P(("z", "x"), ("y", "c"), None)
    down = P(("z", "x"), None, ("y", "c"))
    return jax.shard_map(
        work,
        mesh=fine,
        in_specs=(rows, rows, rows, rows, P(), gate_up, down),
        out_specs=(rows, gate_up, down),
        check_vma=False,
    )
```

```python
import functools

import jax
import jax.numpy as jnp
from jax import lax
from jax.experimental import pallas as pl
from jax.experimental.pallas import tpu as pltpu
from jax.sharding import Mesh, PartitionSpec as P


CAP = 4
EPS = 1e-06
Y, C, Z, X = 4, 2, 16, 4
GROUPS = 8
HID = 128
D = 4096
HALF = D // 2
CUT = 512
WIDE = 2 * CUT
ROWS = 2 * Z * X * CAP
F32 = jnp.float32
BF16 = jnp.bfloat16

SWAP = [
    (c * Z + 2 * e + p, p * Z + 2 * e + c) for c in range(C) for e in range(GROUPS) for p in range(2)
]
FLIP = [(i, i ^ 1) for i in range(Z)]
PLUS = [(i, (i + 1) % X) for i in range(X)]
MINUS = [(i, (i - 1) % X) for i in range(X)]
ORDER = (0, 3, 1, 2)


def shape(dims, kind):
    return jax.ShapeDtypeStruct(dims, kind)


def iota(dims, axis):
    return lax.broadcasted_iota(jnp.int32, dims, axis)


def placing(routes):
    n = routes.shape[1]
    inside = routes < GROUPS
    chosen = jnp.sum(jnp.where(inside, routes, 0), axis=0, keepdims=True)
    present = jnp.sum(inside.astype(jnp.int32), axis=0, keepdims=True) > 0
    onehot = jnp.where((iota((GROUPS, n), 0) == chosen) & present, 1.0, 0.0)
    earlier = jnp.where(iota((n, n), 0) < iota((n, n), 1), 1.0, 0.0)
    rank = jnp.dot(onehot.astype(BF16), earlier.astype(BF16), preferred_element_type=F32)
    slot = jnp.sum(rank * onehot, axis=0, keepdims=True).astype(jnp.int32)
    return jnp.where(present, chosen * CAP + slot, -1)


def send_kernel(routes, gate_w, latent, dout, gain, gate_up, down, out, piece, held):
    piece[:, : 2 * HID] = gate_up[0]
    piece[:, 2 * HID :] = down[0].astype(F32).T.astype(BF16)
    n = routes.shape[1]
    where_to = placing(routes[...])
    weight = jnp.sum(
        jnp.where(routes[...] < GROUPS, gate_w[...], F32(0.0)), axis=0, keepdims=True
    )
    row = iota((2 * GROUPS * CAP, n), 0)
    hit = (row // 8 * CAP + row % CAP) == where_to
    take_in = hit & (row % 8 < CAP)
    take_dy = hit & (row % 8 >= CAP)
    factor = jnp.sum(jnp.where(take_dy, weight, F32(0.0)), axis=1, keepdims=True)
    take_in = jnp.where(take_in, 1.0, 0.0).astype(BF16)
    take_dy = jnp.where(take_dy, 1.0, 0.0).astype(BF16)
    square = jnp.zeros((2 * GROUPS * CAP, 1), F32)
    for d in range(D // CUT):
        cols = pl.ds(d * CUT, CUT)
        x = jnp.dot(take_in, latent[:, cols], preferred_element_type=F32)
        held[:, cols] = x
        square = square + jnp.sum(x * x, axis=1, keepdims=True)
    inverse = lax.rsqrt(square * (1.0 / D) + EPS)
    for d in range(D // CUT):
        cols = pl.ds(d * CUT, CUT)
        y = jnp.dot(take_dy, dout[:, cols], preferred_element_type=F32)
        value = held[:, cols] * inverse * gain[:, cols] + y * factor
        for e in range(GROUPS):
            out[2 * e + d % 2, :, pl.ds(d // 2 * CUT, CUT)] = value[8 * e : 8 * e + 8].astype(BF16)


def send_rows(*args):
    return pl.pallas_call(
        send_kernel,
        out_shape=[shape((Z, 8, HALF), BF16), shape((CUT, 3 * HID), BF16)],
        scratch_shapes=[pltpu.VMEM((2 * GROUPS * CAP, D), F32)],
        name="send_rows",
    )(*args)


def hold_kernel(piece, out):
    out[...] = piece[...]


def hold(piece):
    return pl.pallas_call(hold_kernel, out_shape=shape(piece.shape, BF16), name="hold")(piece)


def home_kernel(routes, latent, gain, home, out, grad):
    n = routes.shape[1]
    where_to = placing(routes[...])
    take = jnp.where(iota((GROUPS * CAP, n), 0) == where_to, 1.0, 0.0).astype(BF16)
    for z in range(Z):
        for y in range(Y):
            cols = pl.ds((2 * y + z % 2) * CUT, CUT)
            grad[pl.ds(z // 2 * CAP, CAP), cols] = home[z, :, pl.ds(y * CUT, CUT)].astype(F32)
    x = jnp.dot(take, latent[...], preferred_element_type=F32)
    inverse = lax.rsqrt(jnp.sum(x * x, axis=1, keepdims=True) * (1.0 / D) + EPS)
    scaled = x * inverse
    g = grad[...] * gain[...]
    mean = jnp.sum(g * scaled, axis=1, keepdims=True) * (1.0 / D)
    value = (inverse * (g - scaled * mean)).astype(BF16)
    out[...] = lax.dot_general(
        take, value, (((0,), (0,)), ((), ())), preferred_element_type=F32
    ).astype(BF16)


def home_rows(routes, latent, gain, home):
    return pl.pallas_call(
        home_kernel,
        out_shape=shape(latent.shape, BF16),
        scratch_shapes=[pltpu.VMEM((GROUPS * CAP, D), F32)],
        name="home_rows",
    )(routes, latent, gain, home)


def turned(value):
    n = value.shape[1]
    tiles = value.reshape(-1, 8, n)
    return pltpu.roll(tiles, 4, 1).reshape(-1, n)


def mix_kernel(count, place, *refs):
    blocks, weights = refs[:count], refs[count]
    mine, other, total = refs[-3:]
    step = pl.program_id(0)
    rows = blocks[0][...]
    if count > 1:
        rows = jnp.concatenate([block[...] for block in blocks], axis=0)
    for g in range(2):
        part = jnp.dot(rows, weights[g], preferred_element_type=F32)

        @pl.when(step == 0)
        def _():
            total[g] = part

        @pl.when(step > 0)
        def _():
            total[g] = total[g] + part

    def packed(both):
        turns = both.reshape(-1, 2, 8, 3 * HID)
        first = turns[:, 0].reshape(-1, 3 * HID)
        second = turns[:, 1].reshape(-1, 3 * HID)
        low = iota((first.shape[0], 2 * HID), 0) % 8 < 4
        pre = jnp.where(low, first[:, : 2 * HID], turned(second[:, : 2 * HID]))
        dh = jnp.where(low[:, :HID], turned(first[:, 2 * HID :]), second[:, 2 * HID :])
        return pre, dh

    @pl.when(step == pl.num_programs(0) - 1)
    def _():
        pre, dh = packed(total[place[0]])
        mine[:, : 2 * HID] = pre
        mine[:, 2 * HID :] = dh
        pre, dh = packed(total[1 - place[0]])
        other[:, : 2 * HID] = pre.astype(BF16)
        other[:, 2 * HID :] = dh.astype(BF16)


def row_specs():
    return [
        pl.BlockSpec((n, WIDE), lambda i, *_: (0, i))
        for n in (ROWS // 4, ROWS // 4, ROWS // 4, ROWS // 8, ROWS // 8)
    ]


def weight_spec():
    return pl.BlockSpec((2, WIDE, 3 * HID), lambda i, *_: (0, i, 0))


def whole(dims):
    return pl.BlockSpec(dims, lambda i, *_: (0,) * len(dims))


def mix(place, blocks, weights):
    rows = sum(block.shape[0] for block in blocks)
    dims = (rows // 2, 3 * HID)
    return pl.pallas_call(
        functools.partial(mix_kernel, len(blocks)),
        grid_spec=pltpu.PrefetchScalarGridSpec(
            num_scalar_prefetch=1,
            grid=(HALF // WIDE,),
            in_specs=[
                *[pl.BlockSpec((b.shape[0], WIDE), lambda i, *_: (0, i)) for b in blocks],
                weight_spec(),
            ],
            out_specs=[whole(dims), whole(dims)],
            scratch_shapes=[pltpu.VMEM((2, rows, 3 * HID), F32)],
        ),
        out_shape=[shape(dims, F32), shape(dims, BF16)],
    )(place, *blocks, weights)


def gates(total):
    gate = total[:, :HID]
    up = total[:, HID : 2 * HID]
    dh = total[:, 2 * HID :]
    sig = jax.nn.sigmoid(gate)
    act = gate * sig
    d_gate = dh * up * sig * (1.0 + gate * (1.0 - sig))
    return jnp.concatenate([d_gate, dh * act, act * up], axis=1).astype(BF16)


def back_kernel(place, mine, other, weights, out, inner):
    @pl.when(pl.program_id(0) == 0)
    def _():
        inner[place[0]] = mine[...]
        inner[1 - place[0]] = other[...]

    total = sum(
        lax.dot_general(
            inner[g, :, : 2 * HID],
            weights[g, :, : 2 * HID],
            (((1,), (1,)), ((), ())),
            preferred_element_type=F32,
        )
        for g in range(2)
    ).astype(BF16)
    n = ROWS // 8
    for k, off in enumerate(ORDER):
        out[lax.rem(place[1] + off, X)] = total[n * k : n * k + n]


def back(place, mine, other, weights):
    dims = (ROWS // 2, 3 * HID)
    return pl.pallas_call(
        back_kernel,
        grid_spec=pltpu.PrefetchScalarGridSpec(
            num_scalar_prefetch=1,
            grid=(HALF // WIDE,),
            in_specs=[whole(dims), whole(dims), weight_spec()],
            out_specs=pl.BlockSpec((X, ROWS // 8, WIDE), lambda i, *_: (0, 0, i)),
            scratch_shapes=[pltpu.VMEM((2, *dims), BF16)],
        ),
        out_shape=shape((X, ROWS // 8, HALF), BF16),
        name="back",
    )(place, mine, other, weights)


def grads_kernel(place, value, own, left, right, far_a, far_b, *refs):
    out, inner = refs[-2:]

    @pl.when(pl.program_id(0) == 0)
    def _():
        both = value[...].astype(F32)
        low = iota((ROWS // 2, 2 * HID), 0) % 8 < 4
        pre = both[:, : 2 * HID]
        hid = both[:, 2 * HID :]
        zero = F32(0.0)
        first = jnp.where(low, pre, zero), jnp.where(low[:, :HID], zero, turned(hid))
        second = jnp.where(low, turned(pre), zero), jnp.where(low[:, :HID], zero, hid)
        for k, cols in ((0, pl.ds(0, 2 * HID)), (1, pl.ds(2 * HID, HID))):
            width = first[k].shape[1]
            pair = jnp.stack(
                [first[k].reshape(-1, 8, width), second[k].reshape(-1, 8, width)], axis=1
            )
            inner[:, cols] = pair.reshape(ROWS, width).astype(BF16)

    rows = jnp.concatenate([own[...], left[...], right[...], far_a[...], far_b[...]], axis=0)
    total = lax.dot_general(
        rows, inner[...], (((0,), (0,)), ((), ())), preferred_element_type=F32
    ).astype(BF16)
    for k in range(WIDE // CUT):
        out[0, k] = total[k * CUT : (k + 1) * CUT]


def grads(place, turn, value, blocks, so_far):
    hold = [pl.BlockSpec(memory_space=pl.ANY)] * len(so_far)

    def at(i, place):
        slot = place[2]
        return (slot if turn == 0 else 1 - slot), i, 0, 0

    return pl.pallas_call(
        grads_kernel,
        grid_spec=pltpu.PrefetchScalarGridSpec(
            num_scalar_prefetch=1,
            grid=(HALF // WIDE,),
            in_specs=[whole((ROWS // 2, 3 * HID)), *row_specs(), *hold],
            out_specs=pl.BlockSpec((1, WIDE // CUT, CUT, 3 * HID), at),
            scratch_shapes=[pltpu.VMEM((ROWS, 3 * HID), BF16)],
        ),
        out_shape=shape((2, HALF // CUT, CUT, 3 * HID), BF16),
        input_output_aliases={2 + len(blocks): 0} if so_far else {},
    )(place, value, *blocks, *so_far)


def work(latent, dout, routes, gate_w, norm_gain, w_gate_up, w_down):
    zp = lax.axis_index("z") % 2
    core = lax.axis_index("c")
    place = jnp.stack([zp, lax.axis_index("x"), (zp + core) % 2]).astype(jnp.int32)
    gain = norm_gain[None, :]
    routes = routes.T

    send, piece = send_rows(routes, gate_w.T, latent, dout, gain, w_gate_up, w_down)
    piece = lax.ppermute(piece, ("c", "z"), SWAP)
    got = lax.all_to_all(send, "z", 0, 0, tiled=True)
    weights = lax.all_gather(hold(piece), ("c", "y"), axis=0, tiled=True)
    weights = weights.reshape(2, HALF, 3 * HID)

    own = got.reshape(ROWS // 4, HALF)
    half = own.shape[0] // 2
    left = lax.ppermute(own, "x", PLUS)
    right = lax.ppermute(own, "x", MINUS)
    far_a = lax.ppermute(left[:half], "x", PLUS)
    far_b = lax.ppermute(right[half:], "x", MINUS)
    blocks = own, left, right, far_a, far_b

    totals = []
    for some in (blocks[:3], blocks[3:]):
        mine, other = mix(place, some, weights)
        got = lax.ppermute(other, "z", FLIP)
        totals.append(mine + got.astype(F32))
    inner = gates(jnp.concatenate(totals, axis=0))
    outer = lax.ppermute(inner, "z", FLIP)

    grad = grads(place, 0, inner, blocks, ())
    grad = grads(place, 1, outer, blocks, (grad,))
    partner = lax.ppermute(grad[1], "c", [(0, 1), (1, 0)])
    part = back(place, inner, outer, weights)
    part = lax.all_to_all(part, "x", 0, 0, tiled=True)
    grad = (grad[0].astype(F32) + partner.astype(F32)).astype(BF16).reshape(HALF, 3 * HID)
    grad = lax.psum_scatter(grad, "y", scatter_dimension=0, tiled=True)
    grad = lax.ppermute(grad, ("c", "z"), SWAP)
    grad_gu = grad[:, : 2 * HID][None]
    grad_d = grad[:, 2 * HID :].T[None]

    summed = jnp.sum(part.astype(F32), axis=0).astype(BF16)
    home = lax.all_to_all(summed.reshape(Z, CAP, HALF), "z", 0, 0, tiled=True)
    return home_rows(routes, latent, gain, home), grad_gu, grad_d


def solution(mesh):
    fine = Mesh(mesh.devices.reshape(Y, C, Z, X), ("y", "c", "z", "x"))
    rows = P(("y", "c", "z", "x"), None)
    gate_up = P(("z", "x"), ("y", "c"), None)
    down = P(("z", "x"), None, ("y", "c"))
    return jax.shard_map(
        work,
        mesh=fine,
        in_specs=(rows, rows, rows, rows, P(), gate_up, down),
        out_specs=(rows, gate_up, down),
        check_vma=False,
    )
```

```python
import functools

import jax
import jax.numpy as jnp
from jax import lax
from jax.experimental import pallas as pl
from jax.experimental.pallas import tpu as pltpu
from jax.sharding import Mesh, PartitionSpec as P


CAP = 4
EPS = 1e-06
Y, C, Z, X = 4, 2, 16, 4
GROUPS = 8
HID = 128
D = 4096
HALF = D // 2
CUT = 512
WIDE = 2 * CUT
ROWS = 2 * Z * X * CAP
F32 = jnp.float32
BF16 = jnp.bfloat16

SWAP = [
    (c * Z + 2 * e + p, p * Z + 2 * e + c) for c in range(C) for e in range(GROUPS) for p in range(2)
]
FLIP = [(i, i ^ 1) for i in range(Z)]
PLUS = [(i, (i + 1) % X) for i in range(X)]
MINUS = [(i, (i - 1) % X) for i in range(X)]
ORDER = (0, 3, 1, 2)


def shape(dims, kind):
    return jax.ShapeDtypeStruct(dims, kind)


def iota(dims, axis):
    return lax.broadcasted_iota(jnp.int32, dims, axis)


def placing(routes):
    n = routes.shape[1]
    inside = routes < GROUPS
    chosen = jnp.sum(jnp.where(inside, routes, 0), axis=0, keepdims=True)
    present = jnp.sum(inside.astype(jnp.int32), axis=0, keepdims=True) > 0
    onehot = jnp.where((iota((GROUPS, n), 0) == chosen) & present, 1.0, 0.0)
    earlier = jnp.where(iota((n, n), 0) < iota((n, n), 1), 1.0, 0.0)
    rank = jnp.dot(onehot.astype(BF16), earlier.astype(BF16), preferred_element_type=F32)
    slot = jnp.sum(rank * onehot, axis=0, keepdims=True).astype(jnp.int32)
    return jnp.where(present, chosen * CAP + slot, -1)


def send_kernel(routes, gate_w, latent, dout, gain, gate_up, down, out, piece, held):
    piece[:, : 2 * HID] = gate_up[0]
    piece[:, 2 * HID :] = down[0].astype(F32).T.astype(BF16)
    n = routes.shape[1]
    where_to = placing(routes[...])
    weight = jnp.sum(
        jnp.where(routes[...] < GROUPS, gate_w[...], F32(0.0)), axis=0, keepdims=True
    )
    row = iota((2 * GROUPS * CAP, n), 0)
    hit = (row // 8 * CAP + row % CAP) == where_to
    take_in = hit & (row % 8 < CAP)
    take_dy = hit & (row % 8 >= CAP)
    factor = jnp.sum(jnp.where(take_dy, weight, F32(0.0)), axis=1, keepdims=True)
    take_in = jnp.where(take_in, 1.0, 0.0).astype(BF16)
    take_dy = jnp.where(take_dy, 1.0, 0.0).astype(BF16)
    square = jnp.zeros((2 * GROUPS * CAP, 1), F32)
    for d in range(D // CUT):
        cols = pl.ds(d * CUT, CUT)
        x = jnp.dot(take_in, latent[:, cols], preferred_element_type=F32)
        held[:, cols] = x
        square = square + jnp.sum(x * x, axis=1, keepdims=True)
    inverse = lax.rsqrt(square * (1.0 / D) + EPS)
    for d in range(D // CUT):
        cols = pl.ds(d * CUT, CUT)
        y = jnp.dot(take_dy, dout[:, cols], preferred_element_type=F32)
        value = held[:, cols] * inverse * gain[:, cols] + y * factor
        for e in range(GROUPS):
            out[2 * e + d % 2, :, pl.ds(d // 2 * CUT, CUT)] = value[8 * e : 8 * e + 8].astype(BF16)


def send_rows(*args):
    return pl.pallas_call(
        send_kernel,
        out_shape=[shape((Z, 8, HALF), BF16), shape((CUT, 3 * HID), BF16)],
        scratch_shapes=[pltpu.VMEM((2 * GROUPS * CAP, D), F32)],
        name="send_rows",
    )(*args)


def hold_kernel(piece, out):
    out[...] = piece[...]


def hold(piece):
    return pl.pallas_call(hold_kernel, out_shape=shape(piece.shape, BF16), name="hold")(piece)


def home_kernel(routes, latent, gain, home, out, grad):
    n = routes.shape[1]
    where_to = placing(routes[...])
    take = jnp.where(iota((GROUPS * CAP, n), 0) == where_to, 1.0, 0.0).astype(BF16)
    for z in range(Z):
        for y in range(Y):
            cols = pl.ds((2 * y + z % 2) * CUT, CUT)
            grad[pl.ds(z // 2 * CAP, CAP), cols] = home[z, :, pl.ds(y * CUT, CUT)].astype(F32)
    x = jnp.dot(take, latent[...], preferred_element_type=F32)
    inverse = lax.rsqrt(jnp.sum(x * x, axis=1, keepdims=True) * (1.0 / D) + EPS)
    scaled = x * inverse
    g = grad[...] * gain[...]
    mean = jnp.sum(g * scaled, axis=1, keepdims=True) * (1.0 / D)
    value = (inverse * (g - scaled * mean)).astype(BF16)
    out[...] = lax.dot_general(
        take, value, (((0,), (0,)), ((), ())), preferred_element_type=F32
    ).astype(BF16)


def home_rows(routes, latent, gain, home):
    return pl.pallas_call(
        home_kernel,
        out_shape=shape(latent.shape, BF16),
        scratch_shapes=[pltpu.VMEM((GROUPS * CAP, D), F32)],
        name="home_rows",
    )(routes, latent, gain, home)


def turned(value):
    n = value.shape[1]
    tiles = value.reshape(-1, 8, n)
    return pltpu.roll(tiles, 4, 1).reshape(-1, n)


def mix_kernel(count, place, *refs):
    blocks, weights = refs[:count], refs[count]
    mine, other, total = refs[-3:]
    step = pl.program_id(0)
    rows = blocks[0][...]
    if count > 1:
        rows = jnp.concatenate([block[...] for block in blocks], axis=0)
    for g in range(2):
        part = jnp.dot(rows, weights[g], preferred_element_type=F32)

        @pl.when(step == 0)
        def _():
            total[g] = part

        @pl.when(step > 0)
        def _():
            total[g] = total[g] + part

    def packed(both):
        turns = both.reshape(-1, 2, 8, 3 * HID)
        first = turns[:, 0].reshape(-1, 3 * HID)
        second = turns[:, 1].reshape(-1, 3 * HID)
        low = iota((first.shape[0], 2 * HID), 0) % 8 < 4
        pre = jnp.where(low, first[:, : 2 * HID], turned(second[:, : 2 * HID]))
        dh = jnp.where(low[:, :HID], turned(first[:, 2 * HID :]), second[:, 2 * HID :])
        return pre, dh

    @pl.when(step == pl.num_programs(0) - 1)
    def _():
        pre, dh = packed(total[place[0]])
        mine[:, : 2 * HID] = pre
        mine[:, 2 * HID :] = dh
        pre, dh = packed(total[1 - place[0]])
        other[:, : 2 * HID] = pre.astype(BF16)
        other[:, 2 * HID :] = dh.astype(BF16)


def row_specs():
    return [
        pl.BlockSpec((n, WIDE), lambda i, *_: (0, i))
        for n in (ROWS // 4, ROWS // 4, ROWS // 4, ROWS // 8, ROWS // 8)
    ]


def weight_spec():
    return pl.BlockSpec((2, WIDE, 3 * HID), lambda i, *_: (0, i, 0))


def whole(dims):
    return pl.BlockSpec(dims, lambda i, *_: (0,) * len(dims))


def mix(place, blocks, weights):
    rows = sum(block.shape[0] for block in blocks)
    dims = (rows // 2, 3 * HID)
    return pl.pallas_call(
        functools.partial(mix_kernel, len(blocks)),
        grid_spec=pltpu.PrefetchScalarGridSpec(
            num_scalar_prefetch=1,
            grid=(HALF // WIDE,),
            in_specs=[
                *[pl.BlockSpec((b.shape[0], WIDE), lambda i, *_: (0, i)) for b in blocks],
                weight_spec(),
            ],
            out_specs=[whole(dims), whole(dims)],
            scratch_shapes=[pltpu.VMEM((2, rows, 3 * HID), F32)],
        ),
        out_shape=[shape(dims, F32), shape(dims, BF16)],
    )(place, *blocks, weights)


def gates(total):
    gate = total[:, :HID]
    up = total[:, HID : 2 * HID]
    dh = total[:, 2 * HID :]
    sig = jax.nn.sigmoid(gate)
    act = gate * sig
    d_gate = dh * up * sig * (1.0 + gate * (1.0 - sig))
    return jnp.concatenate([d_gate, dh * act, act * up], axis=1).astype(BF16)


def back_kernel(place, mine, other, weights, out, inner):
    @pl.when(pl.program_id(0) == 0)
    def _():
        inner[place[0]] = mine[...]
        inner[1 - place[0]] = other[...]

    total = sum(
        lax.dot_general(
            inner[g, :, : 2 * HID],
            weights[g, :, : 2 * HID],
            (((1,), (1,)), ((), ())),
            preferred_element_type=F32,
        )
        for g in range(2)
    ).astype(BF16)
    n = ROWS // 8
    for k, off in enumerate(ORDER):
        out[lax.rem(place[1] + off, X)] = total[n * k : n * k + n]


def back(place, mine, other, weights):
    dims = (ROWS // 2, 3 * HID)
    return pl.pallas_call(
        back_kernel,
        grid_spec=pltpu.PrefetchScalarGridSpec(
            num_scalar_prefetch=1,
            grid=(HALF // WIDE,),
            in_specs=[whole(dims), whole(dims), weight_spec()],
            out_specs=pl.BlockSpec((X, ROWS // 8, WIDE), lambda i, *_: (0, 0, i)),
            scratch_shapes=[pltpu.VMEM((2, *dims), BF16)],
        ),
        out_shape=shape((X, ROWS // 8, HALF), BF16),
        name="back",
    )(place, mine, other, weights)


def grads_kernel(kept, place, mine, other, own, left, right, far_a, far_b, *refs):
    out, inner = refs[-2:]

    @pl.when(pl.program_id(0) == 0)
    def _():
        is_mine = place[2] == (0 if kept else 1)
        both = jnp.where(is_mine, mine[...].astype(F32), other[...].astype(F32))
        low = iota((ROWS // 2, 2 * HID), 0) % 8 < 4
        pre = both[:, : 2 * HID]
        hid = both[:, 2 * HID :]
        zero = F32(0.0)
        first = jnp.where(low, pre, zero), jnp.where(low[:, :HID], zero, turned(hid))
        second = jnp.where(low, turned(pre), zero), jnp.where(low[:, :HID], zero, hid)
        for k, cols in ((0, pl.ds(0, 2 * HID)), (1, pl.ds(2 * HID, HID))):
            width = first[k].shape[1]
            pair = jnp.stack(
                [first[k].reshape(-1, 8, width), second[k].reshape(-1, 8, width)], axis=1
            )
            inner[:, cols] = pair.reshape(ROWS, width).astype(BF16)

    rows = jnp.concatenate([own[...], left[...], right[...], far_a[...], far_b[...]], axis=0)
    total = lax.dot_general(
        rows, inner[...], (((0,), (0,)), ((), ())), preferred_element_type=F32
    )
    for k in range(WIDE // CUT):
        part = total[k * CUT : (k + 1) * CUT]
        if kept:
            part = part + refs[0][k].astype(F32)
        out[k] = part.astype(BF16)


def grads(place, mine, other, blocks, received):
    dims = (ROWS // 2, 3 * HID)
    part = pl.BlockSpec((WIDE // CUT, CUT, 3 * HID), lambda i, *_: (i, 0, 0))
    return pl.pallas_call(
        functools.partial(grads_kernel, len(received)),
        grid_spec=pltpu.PrefetchScalarGridSpec(
            num_scalar_prefetch=1,
            grid=(HALF // WIDE,),
            in_specs=[whole(dims), whole(dims), *row_specs(), *[part for _ in received]],
            out_specs=part,
            scratch_shapes=[pltpu.VMEM((ROWS, 3 * HID), BF16)],
        ),
        out_shape=shape((HALF // CUT, CUT, 3 * HID), BF16),
    )(place, mine, other, *blocks, *received)


def work(latent, dout, routes, gate_w, norm_gain, w_gate_up, w_down):
    zp = lax.axis_index("z") % 2
    core = lax.axis_index("c")
    place = jnp.stack([zp, lax.axis_index("x"), (zp + core) % 2]).astype(jnp.int32)
    gain = norm_gain[None, :]
    routes = routes.T

    send, piece = send_rows(routes, gate_w.T, latent, dout, gain, w_gate_up, w_down)
    piece = lax.ppermute(piece, ("c", "z"), SWAP)
    got = lax.all_to_all(send, "z", 0, 0, tiled=True)
    weights = lax.all_gather(hold(piece), ("c", "y"), axis=0, tiled=True)
    weights = weights.reshape(2, HALF, 3 * HID)

    own = got.reshape(ROWS // 4, HALF)
    half = own.shape[0] // 2
    left = lax.ppermute(own, "x", PLUS)
    right = lax.ppermute(own, "x", MINUS)
    far_a = lax.ppermute(left[:half], "x", PLUS)
    far_b = lax.ppermute(right[half:], "x", MINUS)
    blocks = own, left, right, far_a, far_b

    totals = []
    for some in (blocks[:3], blocks[3:]):
        mine, other = mix(place, some, weights)
        got = lax.ppermute(other, "z", FLIP)
        totals.append(mine + got.astype(F32))
    inner = gates(jnp.concatenate(totals, axis=0))
    outer = lax.ppermute(inner, "z", FLIP)

    received = lax.ppermute(grads(place, inner, outer, blocks, ()), "c", [(0, 1), (1, 0)])
    part = back(place, inner, outer, weights)
    part = lax.all_to_all(part, "x", 0, 0, tiled=True)
    grad = grads(place, inner, outer, blocks, (received,)).reshape(HALF, 3 * HID)
    grad = lax.psum_scatter(grad, "y", scatter_dimension=0, tiled=True)
    grad = lax.ppermute(grad, ("c", "z"), SWAP)
    grad_gu = grad[:, : 2 * HID][None]
    grad_d = grad[:, 2 * HID :].T[None]

    summed = jnp.sum(part.astype(F32), axis=0).astype(BF16)
    home = lax.all_to_all(summed.reshape(Z, CAP, HALF), "z", 0, 0, tiled=True)
    return home_rows(routes, latent, gain, home), grad_gu, grad_d


def solution(mesh):
    fine = Mesh(mesh.devices.reshape(Y, C, Z, X), ("y", "c", "z", "x"))
    rows = P(("y", "c", "z", "x"), None)
    gate_up = P(("z", "x"), ("y", "c"), None)
    down = P(("z", "x"), None, ("y", "c"))
    return jax.shard_map(
        work,
        mesh=fine,
        in_specs=(rows, rows, rows, rows, P(), gate_up, down),
        out_specs=(rows, gate_up, down),
        check_vma=False,
    )
```

```python
import functools

import jax
import jax.numpy as jnp
from jax import lax
from jax.experimental import pallas as pl
from jax.experimental.pallas import tpu as pltpu
from jax.sharding import Mesh, PartitionSpec as P


CAP = 4
EPS = 1e-06
Y, C, Z, X = 4, 2, 16, 4
GROUPS = 8
HID = 128
D = 4096
HALF = D // 2
CUT = 512
WIDE = 2 * CUT
ROWS = 2 * Z * X * CAP
F32 = jnp.float32
BF16 = jnp.bfloat16

SWAP = [
    (c * Z + 2 * e + p, p * Z + 2 * e + c) for c in range(C) for e in range(GROUPS) for p in range(2)
]
FLIP = [(i, i ^ 1) for i in range(Z)]
PLUS = [(i, (i + 1) % X) for i in range(X)]
MINUS = [(i, (i - 1) % X) for i in range(X)]
TURN = [(0, 1), (1, 0)]
ORDER = (0, 3, 1, 2)


def shape(dims, kind):
    return jax.ShapeDtypeStruct(dims, kind)


def iota(dims, axis):
    return lax.broadcasted_iota(jnp.int32, dims, axis)


def placing(routes):
    n = routes.shape[1]
    inside = routes < GROUPS
    chosen = jnp.sum(jnp.where(inside, routes, 0), axis=0, keepdims=True)
    present = jnp.sum(inside.astype(jnp.int32), axis=0, keepdims=True) > 0
    onehot = jnp.where((iota((GROUPS, n), 0) == chosen) & present, 1.0, 0.0)
    earlier = jnp.where(iota((n, n), 0) < iota((n, n), 1), 1.0, 0.0)
    rank = jnp.dot(onehot.astype(BF16), earlier.astype(BF16), preferred_element_type=F32)
    slot = jnp.sum(rank * onehot, axis=0, keepdims=True).astype(jnp.int32)
    return jnp.where(present, chosen * CAP + slot, -1)


def send_kernel(routes, gate_w, latent, dout, gain, gate_up, down, out, piece, held):
    piece[:, : 2 * HID] = gate_up[0]
    piece[:, 2 * HID :] = down[0].astype(F32).T.astype(BF16)
    n = routes.shape[1]
    where_to = placing(routes[...])
    weight = jnp.sum(
        jnp.where(routes[...] < GROUPS, gate_w[...], F32(0.0)), axis=0, keepdims=True
    )
    row = iota((2 * GROUPS * CAP, n), 0)
    hit = (row // 8 * CAP + row % CAP) == where_to
    take_in = hit & (row % 8 < CAP)
    take_dy = hit & (row % 8 >= CAP)
    factor = jnp.sum(jnp.where(take_dy, weight, F32(0.0)), axis=1, keepdims=True)
    take_in = jnp.where(take_in, 1.0, 0.0).astype(BF16)
    take_dy = jnp.where(take_dy, 1.0, 0.0).astype(BF16)
    square = jnp.zeros((2 * GROUPS * CAP, 1), F32)
    for d in range(D // CUT):
        cols = pl.ds(d * CUT, CUT)
        x = jnp.dot(take_in, latent[:, cols], preferred_element_type=F32)
        held[:, cols] = x
        square = square + jnp.sum(x * x, axis=1, keepdims=True)
    inverse = lax.rsqrt(square * (1.0 / D) + EPS)
    for d in range(D // CUT):
        cols = pl.ds(d * CUT, CUT)
        y = jnp.dot(take_dy, dout[:, cols], preferred_element_type=F32)
        value = held[:, cols] * inverse * gain[:, cols] + y * factor
        for e in range(GROUPS):
            out[2 * e + d % 2, :, pl.ds(d // 2 * CUT, CUT)] = value[8 * e : 8 * e + 8].astype(BF16)


def send_rows(*args):
    return pl.pallas_call(
        send_kernel,
        out_shape=[shape((Z, 8, HALF), BF16), shape((CUT, 3 * HID), BF16)],
        scratch_shapes=[pltpu.VMEM((2 * GROUPS * CAP, D), F32)],
        name="send_rows",
    )(*args)


def join_kernel(place, own, left, right, far_a, far_b, out):
    half = CUT // 2
    for block, k, first in ((own, 0, 0), (left, 1, 0), (right, 2, 0), (far_a, 3, 0), (far_b, 3, half)):
        at = pl.multiple_of(place[7 + k] * CUT + first, half)
        out[pl.ds(at, block.shape[0]), :] = block[...]


def join(place, blocks):
    return pl.pallas_call(
        join_kernel,
        grid_spec=pltpu.PrefetchScalarGridSpec(
            num_scalar_prefetch=1,
            grid=(1,),
            in_specs=[whole(block.shape) for block in blocks],
            out_specs=whole((HALF, 3 * HID)),
        ),
        out_shape=shape((HALF, 3 * HID), BF16),
        name="join",
    )(place, *blocks)


def home_kernel(routes, latent, gain, home, out, grad):
    n = routes.shape[1]
    where_to = placing(routes[...])
    take = jnp.where(iota((GROUPS * CAP, n), 0) == where_to, 1.0, 0.0).astype(BF16)
    for z in range(Z):
        for y in range(Y):
            cols = pl.ds((2 * y + z % 2) * CUT, CUT)
            grad[pl.ds(z // 2 * CAP, CAP), cols] = home[z, :, pl.ds(y * CUT, CUT)].astype(F32)
    x = jnp.dot(take, latent[...], preferred_element_type=F32)
    inverse = lax.rsqrt(jnp.sum(x * x, axis=1, keepdims=True) * (1.0 / D) + EPS)
    scaled = x * inverse
    g = grad[...] * gain[...]
    mean = jnp.sum(g * scaled, axis=1, keepdims=True) * (1.0 / D)
    value = (inverse * (g - scaled * mean)).astype(BF16)
    out[...] = lax.dot_general(
        take, value, (((0,), (0,)), ((), ())), preferred_element_type=F32
    ).astype(BF16)


def home_rows(routes, latent, gain, home):
    return pl.pallas_call(
        home_kernel,
        out_shape=shape(latent.shape, BF16),
        scratch_shapes=[pltpu.VMEM((GROUPS * CAP, D), F32)],
        name="home_rows",
    )(routes, latent, gain, home)


def turned(value):
    n = value.shape[1]
    tiles = value.reshape(-1, 8, n)
    return pltpu.roll(tiles, 4, 1).reshape(-1, n)


def mix_kernel(count, place, *refs):
    blocks, weights = refs[:count], refs[count : count + 2]
    mine, other, total = refs[-3:]
    step = pl.program_id(0)
    rows = blocks[0][...]
    if count > 1:
        rows = jnp.concatenate([block[...] for block in blocks], axis=0)
    for g in range(2):
        part = jnp.dot(rows, weights[g][...], preferred_element_type=F32)

        @pl.when(step == 0)
        def _():
            total[g] = part

        @pl.when(step > 0)
        def _():
            total[g] = total[g] + part

    def packed(both):
        turns = both.reshape(-1, 2, 8, 3 * HID)
        first = turns[:, 0].reshape(-1, 3 * HID)
        second = turns[:, 1].reshape(-1, 3 * HID)
        low = iota((first.shape[0], 2 * HID), 0) % 8 < 4
        pre = jnp.where(low, first[:, : 2 * HID], turned(second[:, : 2 * HID]))
        dh = jnp.where(low[:, :HID], turned(first[:, 2 * HID :]), second[:, 2 * HID :])
        return pre, dh

    @pl.when(step == pl.num_programs(0) - 1)
    def _():
        pre, dh = packed(total[place[2]])
        mine[:, : 2 * HID] = pre
        mine[:, 2 * HID :] = dh
        pre, dh = packed(total[1 - place[2]])
        other[:, : 2 * HID] = pre.astype(BF16)
        other[:, 2 * HID :] = dh.astype(BF16)


def row_specs():
    return [
        pl.BlockSpec((n, WIDE), lambda i, *_: (0, i))
        for n in (ROWS // 4, ROWS // 4, ROWS // 4, ROWS // 8, ROWS // 8)
    ]


def weight_specs():
    return [pl.BlockSpec((WIDE, 3 * HID), lambda i, *_: (i, 0))] * 2


def whole(dims):
    return pl.BlockSpec(dims, lambda i, *_: (0,) * len(dims))


def mix(place, blocks, weights):
    rows = sum(block.shape[0] for block in blocks)
    dims = (rows // 2, 3 * HID)
    return pl.pallas_call(
        functools.partial(mix_kernel, len(blocks)),
        grid_spec=pltpu.PrefetchScalarGridSpec(
            num_scalar_prefetch=1,
            grid=(HALF // WIDE,),
            in_specs=[
                *[pl.BlockSpec((b.shape[0], WIDE), lambda i, *_: (0, i)) for b in blocks],
                *weight_specs(),
            ],
            out_specs=[whole(dims), whole(dims)],
            scratch_shapes=[pltpu.VMEM((2, rows, 3 * HID), F32)],
        ),
        out_shape=[shape(dims, F32), shape(dims, BF16)],
    )(place, *blocks, *weights)


def gates(total):
    gate = total[:, :HID]
    up = total[:, HID : 2 * HID]
    dh = total[:, 2 * HID :]
    sig = jax.nn.sigmoid(gate)
    act = gate * sig
    d_gate = dh * up * sig * (1.0 + gate * (1.0 - sig))
    return jnp.concatenate([d_gate, dh * act, act * up], axis=1).astype(BF16)


def back_kernel(place, mine, other, weights_a, weights_b, out, inner):
    weights = weights_a, weights_b

    @pl.when(pl.program_id(0) == 0)
    def _():
        inner[place[2]] = mine[...]
        inner[1 - place[2]] = other[...]

    total = sum(
        lax.dot_general(
            inner[g, :, : 2 * HID],
            weights[g][:, : 2 * HID],
            (((1,), (1,)), ((), ())),
            preferred_element_type=F32,
        )
        for g in range(2)
    ).astype(BF16)
    n = ROWS // 8
    for k, off in enumerate(ORDER):
        out[lax.rem(place[1] + off, X)] = total[n * k : n * k + n]


def back(place, mine, other, weights):
    dims = (ROWS // 2, 3 * HID)
    return pl.pallas_call(
        back_kernel,
        grid_spec=pltpu.PrefetchScalarGridSpec(
            num_scalar_prefetch=1,
            grid=(HALF // WIDE,),
            in_specs=[whole(dims), whole(dims), *weight_specs()],
            out_specs=pl.BlockSpec((X, ROWS // 8, WIDE), lambda i, *_: (0, 0, i)),
            scratch_shapes=[pltpu.VMEM((2, *dims), BF16)],
        ),
        out_shape=shape((X, ROWS // 8, HALF), BF16),
        name="back",
    )(place, mine, other, *weights)


def grads_kernel(kept, place, mine, other, own, left, right, far_a, far_b, *refs):
    out, inner = refs[-2:]

    @pl.when(pl.program_id(0) == 0)
    def _():
        is_mine = place[2] == (0 if kept else 1)
        both = jnp.where(is_mine, mine[...].astype(F32), other[...].astype(F32))
        low = iota((ROWS // 2, 2 * HID), 0) % 8 < 4
        pre = both[:, : 2 * HID]
        hid = both[:, 2 * HID :]
        zero = F32(0.0)
        first = jnp.where(low, pre, zero), jnp.where(low[:, :HID], zero, turned(hid))
        second = jnp.where(low, turned(pre), zero), jnp.where(low[:, :HID], zero, hid)
        for k, cols in ((0, pl.ds(0, 2 * HID)), (1, pl.ds(2 * HID, HID))):
            width = first[k].shape[1]
            pair = jnp.stack(
                [first[k].reshape(-1, 8, width), second[k].reshape(-1, 8, width)], axis=1
            )
            inner[:, cols] = pair.reshape(ROWS, width).astype(BF16)

    rows = jnp.concatenate([own[...], left[...], right[...], far_a[...], far_b[...]], axis=0)
    total = lax.dot_general(
        rows, inner[...], (((0,), (0,)), ((), ())), preferred_element_type=F32
    )
    for k in range(WIDE // CUT):
        part = total[k * CUT : (k + 1) * CUT]
        if kept:
            part = part + refs[0][k].astype(F32)
            out[place[3 + pl.program_id(0) * (WIDE // CUT) + k]] = part.astype(BF16)
        else:
            out[k] = part.astype(BF16)


def grads(place, mine, other, blocks, received):
    dims = (ROWS // 2, 3 * HID)
    part = pl.BlockSpec((WIDE // CUT, CUT, 3 * HID), lambda i, *_: (i, 0, 0))
    return pl.pallas_call(
        functools.partial(grads_kernel, len(received)),
        grid_spec=pltpu.PrefetchScalarGridSpec(
            num_scalar_prefetch=1,
            grid=(HALF // WIDE,),
            in_specs=[whole(dims), whole(dims), *row_specs(), *[part for _ in received]],
            out_specs=whole((HALF // CUT, CUT, 3 * HID)) if received else part,
            scratch_shapes=[pltpu.VMEM((ROWS, 3 * HID), BF16)],
        ),
        out_shape=shape((HALF // CUT, CUT, 3 * HID), BF16),
    )(place, mine, other, *blocks, *received)


def gathered(own, axis):
    half = own.shape[0] // 2
    left = lax.ppermute(own, axis, PLUS)
    right = lax.ppermute(own, axis, MINUS)
    far_a = lax.ppermute(left[:half], axis, PLUS)
    far_b = lax.ppermute(right[half:], axis, MINUS)
    return own, left, right, far_a, far_b


def scattered(parts):
    own, left, right, far = parts
    half = own.shape[0] // 2
    got_a = lax.ppermute(far[:half], "y", MINUS).astype(F32)
    got_b = lax.ppermute(far[half:], "y", PLUS).astype(F32)
    near_a = (left[:half].astype(F32) + got_a).astype(BF16)
    near_b = (right[half:].astype(F32) + got_b).astype(BF16)
    left = jnp.concatenate([near_a, left[half:]], axis=0)
    right = jnp.concatenate([right[:half], near_b], axis=0)
    left = lax.ppermute(left, "y", MINUS)
    right = lax.ppermute(right, "y", PLUS)
    return (own.astype(F32) + left.astype(F32) + right.astype(F32)).astype(BF16)


def work(latent, dout, routes, gate_w, norm_gain, w_gate_up, w_down):
    zp = lax.axis_index("z") % 2
    y = lax.axis_index("y")
    away = (jnp.arange(Y, dtype=jnp.int32) - y) % Y
    ring = jnp.where(away == 0, 0, jnp.where(away == 3, 1, away + 1))
    first = [zp, lax.axis_index("x"), (zp + lax.axis_index("c")) % 2]
    place = jnp.concatenate(
        [jnp.stack(first), ring, jnp.stack([(y + off) % Y for off in ORDER])]
    ).astype(jnp.int32)
    gain = norm_gain[None, :]
    routes = routes.T

    send, piece = send_rows(routes, gate_w.T, latent, dout, gain, w_gate_up, w_down)
    piece = lax.ppermute(piece, ("c", "z"), SWAP)
    got = lax.all_to_all(send, "z", 0, 0, tiled=True)
    joined = join(place, gathered(piece, "y"))
    weights = joined, lax.ppermute(joined, "c", TURN)
    blocks = gathered(got.reshape(ROWS // 4, HALF), "x")

    totals = []
    for some in (blocks[:3], blocks[3:]):
        mine, other = mix(place, some, weights)
        got = lax.ppermute(other, "z", FLIP)
        totals.append(mine + got.astype(F32))
    inner = gates(jnp.concatenate(totals, axis=0))
    outer = lax.ppermute(inner, "z", FLIP)

    part = back(place, inner, outer, weights)
    part = lax.all_to_all(part, "x", 0, 0, tiled=True)
    received = lax.ppermute(grads(place, inner, outer, blocks, ()), "c", TURN)
    grad = scattered(grads(place, inner, outer, blocks, (received,)))
    grad = lax.ppermute(grad, ("c", "z"), SWAP)
    grad_gu = grad[:, : 2 * HID][None]
    grad_d = grad[:, 2 * HID :].T[None]

    summed = jnp.sum(part.astype(F32), axis=0).astype(BF16)
    home = lax.all_to_all(summed.reshape(Z, CAP, HALF), "z", 0, 0, tiled=True)
    return home_rows(routes, latent, gain, home), grad_gu, grad_d


def solution(mesh):
    fine = Mesh(mesh.devices.reshape(Y, C, Z, X), ("y", "c", "z", "x"))
    rows = P(("y", "c", "z", "x"), None)
    gate_up = P(("z", "x"), ("y", "c"), None)
    down = P(("z", "x"), None, ("y", "c"))
    return jax.shard_map(
        work,
        mesh=fine,
        in_specs=(rows, rows, rows, rows, P(), gate_up, down),
        out_specs=(rows, gate_up, down),
        check_vma=False,
    )
```

```python
import functools

import jax
import jax.numpy as jnp
from jax import lax
from jax.experimental import pallas as pl
from jax.experimental.pallas import tpu as pltpu
from jax.sharding import Mesh, PartitionSpec as P


CAP = 4
EPS = 1e-06
Y, C, Z, X = 4, 2, 16, 4
GROUPS = 8
HID = 128
D = 4096
HALF = D // 2
CUT = 512
WIDE = 2 * CUT
ROWS = 2 * Z * X * CAP
F32 = jnp.float32
BF16 = jnp.bfloat16

SWAP = [
    (c * Z + 2 * e + p, p * Z + 2 * e + c) for c in range(C) for e in range(GROUPS) for p in range(2)
]
FLIP = [(i, i ^ 1) for i in range(Z)]
PLUS = [(i, (i + 1) % X) for i in range(X)]
MINUS = [(i, (i - 1) % X) for i in range(X)]
TURN = [(0, 1), (1, 0)]
ORDER = (0, 3, 1, 2)


def shape(dims, kind):
    return jax.ShapeDtypeStruct(dims, kind)


def iota(dims, axis):
    return lax.broadcasted_iota(jnp.int32, dims, axis)


def placing(routes):
    n = routes.shape[1]
    inside = routes < GROUPS
    chosen = jnp.sum(jnp.where(inside, routes, 0), axis=0, keepdims=True)
    present = jnp.sum(inside.astype(jnp.int32), axis=0, keepdims=True) > 0
    onehot = jnp.where((iota((GROUPS, n), 0) == chosen) & present, 1.0, 0.0)
    earlier = jnp.where(iota((n, n), 0) < iota((n, n), 1), 1.0, 0.0)
    rank = jnp.dot(onehot.astype(BF16), earlier.astype(BF16), preferred_element_type=F32)
    slot = jnp.sum(rank * onehot, axis=0, keepdims=True).astype(jnp.int32)
    return jnp.where(present, chosen * CAP + slot, -1)


def send_kernel(routes, gate_w, latent, dout, gain, gate_up, down, out, piece, held):
    piece[:, : 2 * HID] = gate_up[0]
    piece[:, 2 * HID :] = down[0].astype(F32).T.astype(BF16)
    n = routes.shape[1]
    where_to = placing(routes[...])
    weight = jnp.sum(
        jnp.where(routes[...] < GROUPS, gate_w[...], F32(0.0)), axis=0, keepdims=True
    )
    row = iota((2 * GROUPS * CAP, n), 0)
    hit = (row // 8 * CAP + row % CAP) == where_to
    take_in = hit & (row % 8 < CAP)
    take_dy = hit & (row % 8 >= CAP)
    factor = jnp.sum(jnp.where(take_dy, weight, F32(0.0)), axis=1, keepdims=True)
    take_in = jnp.where(take_in, 1.0, 0.0).astype(BF16)
    take_dy = jnp.where(take_dy, 1.0, 0.0).astype(BF16)
    square = jnp.zeros((2 * GROUPS * CAP, 1), F32)
    for d in range(D // CUT):
        cols = pl.ds(d * CUT, CUT)
        x = jnp.dot(take_in, latent[:, cols], preferred_element_type=F32)
        held[:, cols] = x
        square = square + jnp.sum(x * x, axis=1, keepdims=True)
    inverse = lax.rsqrt(square * (1.0 / D) + EPS)
    for d in range(D // CUT):
        cols = pl.ds(d * CUT, CUT)
        y = jnp.dot(take_dy, dout[:, cols], preferred_element_type=F32)
        value = held[:, cols] * inverse * gain[:, cols] + y * factor
        for e in range(GROUPS):
            out[2 * e + d % 2, :, pl.ds(d // 2 * CUT, CUT)] = value[8 * e : 8 * e + 8].astype(BF16)


def send_rows(*args):
    return pl.pallas_call(
        send_kernel,
        out_shape=[shape((Z, 8, HALF), BF16), shape((CUT, 3 * HID), BF16)],
        scratch_shapes=[pltpu.VMEM((2 * GROUPS * CAP, D), F32)],
        name="send_rows",
    )(*args)


def join_kernel(place, own, left, right, far_a, far_b, out):
    half = CUT // 2
    for block, k, first in ((own, 0, 0), (left, 1, 0), (right, 2, 0), (far_a, 3, 0), (far_b, 3, half)):
        at = pl.multiple_of(place[7 + k] * CUT + first, half)
        out[pl.ds(at, block.shape[0]), :] = block[...]


def join(place, blocks):
    return pl.pallas_call(
        join_kernel,
        grid_spec=pltpu.PrefetchScalarGridSpec(
            num_scalar_prefetch=1,
            grid=(1,),
            in_specs=[whole(block.shape) for block in blocks],
            out_specs=whole((HALF, 3 * HID)),
        ),
        out_shape=shape((HALF, 3 * HID), BF16),
        name="join",
    )(place, *blocks)


def home_kernel(routes, latent, gain, home, out, grad):
    n = routes.shape[1]
    where_to = placing(routes[...])
    take = jnp.where(iota((GROUPS * CAP, n), 0) == where_to, 1.0, 0.0).astype(BF16)
    for z in range(Z):
        for y in range(Y):
            cols = pl.ds((2 * y + z % 2) * CUT, CUT)
            grad[pl.ds(z // 2 * CAP, CAP), cols] = home[z, :, pl.ds(y * CUT, CUT)].astype(F32)
    x = jnp.dot(take, latent[...], preferred_element_type=F32)
    inverse = lax.rsqrt(jnp.sum(x * x, axis=1, keepdims=True) * (1.0 / D) + EPS)
    scaled = x * inverse
    g = grad[...] * gain[...]
    mean = jnp.sum(g * scaled, axis=1, keepdims=True) * (1.0 / D)
    value = (inverse * (g - scaled * mean)).astype(BF16)
    out[...] = lax.dot_general(
        take, value, (((0,), (0,)), ((), ())), preferred_element_type=F32
    ).astype(BF16)


def home_rows(routes, latent, gain, home):
    return pl.pallas_call(
        home_kernel,
        out_shape=shape(latent.shape, BF16),
        scratch_shapes=[pltpu.VMEM((GROUPS * CAP, D), F32)],
        name="home_rows",
    )(routes, latent, gain, home)


def turned(value):
    n = value.shape[1]
    tiles = value.reshape(-1, 8, n)
    return pltpu.roll(tiles, 4, 1).reshape(-1, n)


def mix_kernel(count, place, *refs):
    blocks, weights = refs[:count], refs[count : count + 2]
    mine, other, total = refs[-3:]
    step = pl.program_id(0)
    rows = blocks[0][...]
    if count > 1:
        rows = jnp.concatenate([block[...] for block in blocks], axis=0)
    for g in range(2):
        part = jnp.dot(rows, weights[g][...], preferred_element_type=F32)

        @pl.when(step == 0)
        def _():
            total[g] = part

        @pl.when(step > 0)
        def _():
            total[g] = total[g] + part

    def packed(both):
        turns = both.reshape(-1, 2, 8, 3 * HID)
        first = turns[:, 0].reshape(-1, 3 * HID)
        second = turns[:, 1].reshape(-1, 3 * HID)
        low = iota((first.shape[0], 2 * HID), 0) % 8 < 4
        pre = jnp.where(low, first[:, : 2 * HID], turned(second[:, : 2 * HID]))
        dh = jnp.where(low[:, :HID], turned(first[:, 2 * HID :]), second[:, 2 * HID :])
        return pre, dh

    @pl.when(step == pl.num_programs(0) - 1)
    def _():
        pre, dh = packed(total[place[2]])
        mine[:, : 2 * HID] = pre
        mine[:, 2 * HID :] = dh
        pre, dh = packed(total[1 - place[2]])
        other[:, : 2 * HID] = pre.astype(BF16)
        other[:, 2 * HID :] = dh.astype(BF16)


def row_specs():
    return [
        pl.BlockSpec((n, WIDE), lambda i, *_: (0, i))
        for n in (ROWS // 4, ROWS // 4, ROWS // 4, ROWS // 8, ROWS // 8)
    ]


def weight_specs():
    return [pl.BlockSpec((WIDE, 3 * HID), lambda i, *_: (i, 0))] * 2


def whole(dims):
    return pl.BlockSpec(dims, lambda i, *_: (0,) * len(dims))


def mix(place, blocks, weights):
    rows = sum(block.shape[0] for block in blocks)
    dims = (rows // 2, 3 * HID)
    return pl.pallas_call(
        functools.partial(mix_kernel, len(blocks)),
        grid_spec=pltpu.PrefetchScalarGridSpec(
            num_scalar_prefetch=1,
            grid=(HALF // WIDE,),
            in_specs=[
                *[pl.BlockSpec((b.shape[0], WIDE), lambda i, *_: (0, i)) for b in blocks],
                *weight_specs(),
            ],
            out_specs=[whole(dims), whole(dims)],
            scratch_shapes=[pltpu.VMEM((2, rows, 3 * HID), F32)],
        ),
        out_shape=[shape(dims, F32), shape(dims, BF16)],
    )(place, *blocks, *weights)


def gates(total):
    gate = total[:, :HID]
    up = total[:, HID : 2 * HID]
    dh = total[:, 2 * HID :]
    sig = jax.nn.sigmoid(gate)
    act = gate * sig
    d_gate = dh * up * sig * (1.0 + gate * (1.0 - sig))
    return jnp.concatenate([d_gate, dh * act, act * up], axis=1).astype(BF16)


def back_kernel(place, mine, other, weights_a, weights_b, out, inner):
    weights = weights_a, weights_b

    @pl.when(pl.program_id(0) == 0)
    def _():
        inner[place[2]] = mine[...]
        inner[1 - place[2]] = other[...]

    total = sum(
        lax.dot_general(
            inner[g, :, : 2 * HID],
            weights[g][:, : 2 * HID],
            (((1,), (1,)), ((), ())),
            preferred_element_type=F32,
        )
        for g in range(2)
    ).astype(BF16)
    n = ROWS // 8
    for k, off in enumerate(ORDER):
        out[lax.rem(place[1] + off, X)] = total[n * k : n * k + n]


def back(place, mine, other, weights):
    dims = (ROWS // 2, 3 * HID)
    return pl.pallas_call(
        back_kernel,
        grid_spec=pltpu.PrefetchScalarGridSpec(
            num_scalar_prefetch=1,
            grid=(HALF // WIDE,),
            in_specs=[whole(dims), whole(dims), *weight_specs()],
            out_specs=pl.BlockSpec((X, ROWS // 8, WIDE), lambda i, *_: (0, 0, i)),
            scratch_shapes=[pltpu.VMEM((2, *dims), BF16)],
        ),
        out_shape=shape((X, ROWS // 8, HALF), BF16),
        name="back",
    )(place, mine, other, *weights)


def grads_kernel(kept, place, mine, other, own, left, right, far_a, far_b, *refs):
    out, inner = refs[kept], refs[-1]

    @pl.when(pl.program_id(0) == 0)
    def _():
        is_mine = place[2] == (0 if kept else 1)
        both = jnp.where(is_mine, mine[...].astype(F32), other[...].astype(F32))
        low = iota((ROWS // 2, 2 * HID), 0) % 8 < 4
        pre = both[:, : 2 * HID]
        hid = both[:, 2 * HID :]
        zero = F32(0.0)
        first = jnp.where(low, pre, zero), jnp.where(low[:, :HID], zero, turned(hid))
        second = jnp.where(low, turned(pre), zero), jnp.where(low[:, :HID], zero, hid)
        for k, cols in ((0, pl.ds(0, 2 * HID)), (1, pl.ds(2 * HID, HID))):
            width = first[k].shape[1]
            pair = jnp.stack(
                [first[k].reshape(-1, 8, width), second[k].reshape(-1, 8, width)], axis=1
            )
            inner[:, cols] = pair.reshape(ROWS, width).astype(BF16)

    rows = jnp.concatenate([own[...], left[...], right[...], far_a[...], far_b[...]], axis=0)
    total = lax.dot_general(
        rows, inner[...], (((0,), (0,)), ((), ())), preferred_element_type=F32
    )

    def store(at, value):
        for i, near in enumerate(refs[1:4]):

            @pl.when(at == i)
            def _():
                near[...] = value.astype(BF16)

        for i, far in enumerate(refs[4:6]):

            @pl.when(at == 3)
            def _():
                far[...] = value[i * CUT // 2 : (i + 1) * CUT // 2].astype(BF16)

    for k in range(WIDE // CUT):
        part = total[k * CUT : (k + 1) * CUT]
        if kept:
            store(place[3 + pl.program_id(0) * (WIDE // CUT) + k], part + refs[0][k].astype(F32))
        else:
            out[k] = part.astype(BF16)


def grads(place, mine, other, blocks, received):
    dims = (ROWS // 2, 3 * HID)
    part = pl.BlockSpec((WIDE // CUT, CUT, 3 * HID), lambda i, *_: (i, 0, 0))
    cuts = [(n, 3 * HID) for n in (CUT, CUT, CUT, CUT // 2, CUT // 2)]
    return pl.pallas_call(
        functools.partial(grads_kernel, len(received)),
        grid_spec=pltpu.PrefetchScalarGridSpec(
            num_scalar_prefetch=1,
            grid=(HALF // WIDE,),
            in_specs=[whole(dims), whole(dims), *row_specs(), *[part for _ in received]],
            out_specs=[whole(dims) for dims in cuts] if received else part,
            scratch_shapes=[pltpu.VMEM((ROWS, 3 * HID), BF16)],
        ),
        out_shape=(
            [shape(dims, BF16) for dims in cuts]
            if received
            else shape((HALF // CUT, CUT, 3 * HID), BF16)
        ),
    )(place, mine, other, *blocks, *received)


def gathered(own, axis):
    half = own.shape[0] // 2
    left = lax.ppermute(own, axis, PLUS)
    right = lax.ppermute(own, axis, MINUS)
    far_a = lax.ppermute(left[:half], axis, PLUS)
    far_b = lax.ppermute(right[half:], axis, MINUS)
    return own, left, right, far_a, far_b


def scattered(parts):
    own, left, right, far_a, far_b = parts
    half = own.shape[0] // 2
    got_a = lax.ppermute(far_a, "y", MINUS).astype(F32)
    got_b = lax.ppermute(far_b, "y", PLUS).astype(F32)
    near_a = (left[:half].astype(F32) + got_a).astype(BF16)
    near_b = (right[half:].astype(F32) + got_b).astype(BF16)
    left = jnp.concatenate([near_a, left[half:]], axis=0)
    right = jnp.concatenate([right[:half], near_b], axis=0)
    left = lax.ppermute(left, "y", MINUS)
    right = lax.ppermute(right, "y", PLUS)
    return (own.astype(F32) + left.astype(F32) + right.astype(F32)).astype(BF16)


def work(latent, dout, routes, gate_w, norm_gain, w_gate_up, w_down):
    zp = lax.axis_index("z") % 2
    y = lax.axis_index("y")
    away = (jnp.arange(Y, dtype=jnp.int32) - y) % Y
    ring = jnp.where(away == 0, 0, jnp.where(away == 3, 1, away + 1))
    first = [zp, lax.axis_index("x"), (zp + lax.axis_index("c")) % 2]
    place = jnp.concatenate(
        [jnp.stack(first), ring, jnp.stack([(y + off) % Y for off in ORDER])]
    ).astype(jnp.int32)
    gain = norm_gain[None, :]
    routes = routes.T

    send, piece = send_rows(routes, gate_w.T, latent, dout, gain, w_gate_up, w_down)
    piece = lax.ppermute(piece, ("c", "z"), SWAP)
    got = lax.all_to_all(send, "z", 0, 0, tiled=True)
    joined = join(place, gathered(piece, "y"))
    weights = joined, lax.ppermute(joined, "c", TURN)
    blocks = gathered(got.reshape(ROWS // 4, HALF), "x")

    totals = []
    for some in (blocks[:3], blocks[3:]):
        mine, other = mix(place, some, weights)
        got = lax.ppermute(other, "z", FLIP)
        totals.append(mine + got.astype(F32))
    inner = gates(jnp.concatenate(totals, axis=0))
    outer = lax.ppermute(inner, "z", FLIP)

    sent = grads(place, inner, outer, blocks, ())
    received = lax.ppermute(sent, "c", TURN)
    part = back(place, inner, outer, weights)
    part = lax.all_to_all(part, "x", 0, 0, tiled=True)
    grad = scattered(grads(place, inner, outer, blocks, (received,)))
    grad = lax.ppermute(grad, ("c", "z"), SWAP)
    grad_gu = grad[:, : 2 * HID][None]
    grad_d = grad[:, 2 * HID :].T[None]

    summed = jnp.sum(part.astype(F32), axis=0).astype(BF16)
    home = lax.all_to_all(summed.reshape(Z, CAP, HALF), "z", 0, 0, tiled=True)
    return home_rows(routes, latent, gain, home), grad_gu, grad_d


def solution(mesh):
    fine = Mesh(mesh.devices.reshape(Y, C, Z, X), ("y", "c", "z", "x"))
    rows = P(("y", "c", "z", "x"), None)
    gate_up = P(("z", "x"), ("y", "c"), None)
    down = P(("z", "x"), None, ("y", "c"))
    return jax.shard_map(
        work,
        mesh=fine,
        in_specs=(rows, rows, rows, rows, P(), gate_up, down),
        out_specs=(rows, gate_up, down),
        check_vma=False,
    )
```

```python
import functools

import jax
import jax.numpy as jnp
from jax import lax
from jax.experimental import pallas as pl
from jax.experimental.pallas import tpu as pltpu
from jax.sharding import Mesh, PartitionSpec as P


CAP = 4
EPS = 1e-06
Y, C, Z, X = 4, 2, 16, 4
GROUPS = 8
HID = 128
D = 4096
HALF = D // 2
CUT = 512
WIDE = 2 * CUT
ROWS = 2 * Z * X * CAP
F32 = jnp.float32
BF16 = jnp.bfloat16

SWAP = [
    (c * Z + 2 * e + p, p * Z + 2 * e + c) for c in range(C) for e in range(GROUPS) for p in range(2)
]
FLIP = [(i, i ^ 1) for i in range(Z)]
PLUS = [(i, (i + 1) % X) for i in range(X)]
MINUS = [(i, (i - 1) % X) for i in range(X)]
TURN = [(0, 1), (1, 0)]
ORDER = (0, 3, 1, 2)


def shape(dims, kind):
    return jax.ShapeDtypeStruct(dims, kind)


def iota(dims, axis):
    return lax.broadcasted_iota(jnp.int32, dims, axis)


def placing(routes):
    n = routes.shape[1]
    inside = routes < GROUPS
    chosen = jnp.sum(jnp.where(inside, routes, 0), axis=0, keepdims=True)
    present = jnp.sum(inside.astype(jnp.int32), axis=0, keepdims=True) > 0
    onehot = jnp.where((iota((GROUPS, n), 0) == chosen) & present, 1.0, 0.0)
    earlier = jnp.where(iota((n, n), 0) < iota((n, n), 1), 1.0, 0.0)
    rank = jnp.dot(onehot.astype(BF16), earlier.astype(BF16), preferred_element_type=F32)
    slot = jnp.sum(rank * onehot, axis=0, keepdims=True).astype(jnp.int32)
    return jnp.where(present, chosen * CAP + slot, -1)


def send_kernel(routes, gate_w, latent, dout, gain, gate_up, down, out, piece, held):
    piece[:, : 2 * HID] = gate_up[0]
    piece[:, 2 * HID :] = down[0].astype(F32).T.astype(BF16)
    n = routes.shape[1]
    where_to = placing(routes[...])
    weight = jnp.sum(
        jnp.where(routes[...] < GROUPS, gate_w[...], F32(0.0)), axis=0, keepdims=True
    )
    row = iota((2 * GROUPS * CAP, n), 0)
    hit = (row // 8 * CAP + row % CAP) == where_to
    take_in = hit & (row % 8 < CAP)
    take_dy = hit & (row % 8 >= CAP)
    factor = jnp.sum(jnp.where(take_dy, weight, F32(0.0)), axis=1, keepdims=True)
    take_in = jnp.where(take_in, 1.0, 0.0).astype(BF16)
    take_dy = jnp.where(take_dy, 1.0, 0.0).astype(BF16)
    square = jnp.zeros((2 * GROUPS * CAP, 1), F32)
    for d in range(D // CUT):
        cols = pl.ds(d * CUT, CUT)
        x = jnp.dot(take_in, latent[:, cols], preferred_element_type=F32)
        held[:, cols] = x
        square = square + jnp.sum(x * x, axis=1, keepdims=True)
    inverse = lax.rsqrt(square * (1.0 / D) + EPS)
    for d in range(D // CUT):
        cols = pl.ds(d * CUT, CUT)
        y = jnp.dot(take_dy, dout[:, cols], preferred_element_type=F32)
        value = held[:, cols] * inverse * gain[:, cols] + y * factor
        for e in range(GROUPS):
            out[2 * e + d % 2, :, pl.ds(d // 2 * CUT, CUT)] = value[8 * e : 8 * e + 8].astype(BF16)


def send_rows(*args):
    return pl.pallas_call(
        send_kernel,
        out_shape=[shape((Z, 8, HALF), BF16), shape((CUT, 3 * HID), BF16)],
        scratch_shapes=[pltpu.VMEM((2 * GROUPS * CAP, D), F32)],
        name="send_rows",
    )(*args)


def join_kernel(place, own, left, right, far_a, far_b, out):
    half = CUT // 2
    for block, k, first in ((own, 0, 0), (left, 1, 0), (right, 2, 0), (far_a, 3, 0), (far_b, 3, half)):
        at = pl.multiple_of(place[7 + k] * CUT + first, half)
        out[pl.ds(at, block.shape[0]), :] = block[...]


def join(place, blocks):
    return pl.pallas_call(
        join_kernel,
        grid_spec=pltpu.PrefetchScalarGridSpec(
            num_scalar_prefetch=1,
            grid=(1,),
            in_specs=[whole(block.shape) for block in blocks],
            out_specs=whole((HALF, 3 * HID)),
        ),
        out_shape=shape((HALF, 3 * HID), BF16),
        name="join",
    )(place, *blocks)


def home_kernel(routes, latent, gain, home, out, grad):
    n = routes.shape[1]
    where_to = placing(routes[...])
    take = jnp.where(iota((GROUPS * CAP, n), 0) == where_to, 1.0, 0.0).astype(BF16)
    for z in range(Z):
        for y in range(Y):
            cols = pl.ds((2 * y + z % 2) * CUT, CUT)
            grad[pl.ds(z // 2 * CAP, CAP), cols] = home[z, :, pl.ds(y * CUT, CUT)].astype(F32)
    x = jnp.dot(take, latent[...], preferred_element_type=F32)
    inverse = lax.rsqrt(jnp.sum(x * x, axis=1, keepdims=True) * (1.0 / D) + EPS)
    scaled = x * inverse
    g = grad[...] * gain[...]
    mean = jnp.sum(g * scaled, axis=1, keepdims=True) * (1.0 / D)
    value = (inverse * (g - scaled * mean)).astype(BF16)
    out[...] = lax.dot_general(
        take, value, (((0,), (0,)), ((), ())), preferred_element_type=F32
    ).astype(BF16)


def home_rows(routes, latent, gain, home):
    return pl.pallas_call(
        home_kernel,
        out_shape=shape(latent.shape, BF16),
        scratch_shapes=[pltpu.VMEM((GROUPS * CAP, D), F32)],
        name="home_rows",
    )(routes, latent, gain, home)


def turned(value):
    n = value.shape[1]
    tiles = value.reshape(-1, 8, n)
    return pltpu.roll(tiles, 4, 1).reshape(-1, n)


def mix_kernel(count, place, *refs):
    blocks, weights = refs[:count], refs[count : count + 2]
    mine, other, total = refs[-3:]
    step = pl.program_id(0)
    rows = blocks[0][...]
    if count > 1:
        rows = jnp.concatenate([block[...] for block in blocks], axis=0)
    for g in range(2):
        part = jnp.dot(rows, weights[g][...], preferred_element_type=F32)

        @pl.when(step == 0)
        def _():
            total[g] = part

        @pl.when(step > 0)
        def _():
            total[g] = total[g] + part

    def packed(both):
        turns = both.reshape(-1, 2, 8, 3 * HID)
        first = turns[:, 0].reshape(-1, 3 * HID)
        second = turns[:, 1].reshape(-1, 3 * HID)
        low = iota((first.shape[0], 2 * HID), 0) % 8 < 4
        pre = jnp.where(low, first[:, : 2 * HID], turned(second[:, : 2 * HID]))
        dh = jnp.where(low[:, :HID], turned(first[:, 2 * HID :]), second[:, 2 * HID :])
        return pre, dh

    @pl.when(step == pl.num_programs(0) - 1)
    def _():
        pre, dh = packed(total[place[2]])
        mine[:, : 2 * HID] = pre
        mine[:, 2 * HID :] = dh
        pre, dh = packed(total[1 - place[2]])
        other[:, : 2 * HID] = pre.astype(BF16)
        other[:, 2 * HID :] = dh.astype(BF16)


def row_specs():
    return [
        pl.BlockSpec((n, WIDE), lambda i, *_: (0, i))
        for n in (ROWS // 4, ROWS // 4, ROWS // 4, ROWS // 8, ROWS // 8)
    ]


def weight_specs():
    return [pl.BlockSpec((WIDE, 3 * HID), lambda i, *_: (i, 0))] * 2


def whole(dims):
    return pl.BlockSpec(dims, lambda i, *_: (0,) * len(dims))


def mix(place, blocks, weights):
    rows = sum(block.shape[0] for block in blocks)
    dims = (rows // 2, 3 * HID)
    return pl.pallas_call(
        functools.partial(mix_kernel, len(blocks)),
        grid_spec=pltpu.PrefetchScalarGridSpec(
            num_scalar_prefetch=1,
            grid=(HALF // WIDE,),
            in_specs=[
                *[pl.BlockSpec((b.shape[0], WIDE), lambda i, *_: (0, i)) for b in blocks],
                *weight_specs(),
            ],
            out_specs=[whole(dims), whole(dims)],
            scratch_shapes=[pltpu.VMEM((2, rows, 3 * HID), F32)],
        ),
        out_shape=[shape(dims, F32), shape(dims, BF16)],
    )(place, *blocks, *weights)


def gates(total):
    gate = total[:, :HID]
    up = total[:, HID : 2 * HID]
    dh = total[:, 2 * HID :]
    sig = jax.nn.sigmoid(gate)
    act = gate * sig
    d_gate = dh * up * sig * (1.0 + gate * (1.0 - sig))
    return jnp.concatenate([d_gate, dh * act, act * up], axis=1).astype(BF16)


def back_kernel(place, mine, other, weights_a, weights_b, out, inner):
    weights = weights_a, weights_b

    @pl.when(pl.program_id(0) == 0)
    def _():
        inner[place[2]] = mine[...]
        inner[1 - place[2]] = other[...]

    total = sum(
        lax.dot_general(
            inner[g, :, : 2 * HID],
            weights[g][:, : 2 * HID],
            (((1,), (1,)), ((), ())),
            preferred_element_type=F32,
        )
        for g in range(2)
    ).astype(BF16)
    n = ROWS // 8
    for k, off in enumerate(ORDER):
        out[lax.rem(place[1] + off, X)] = total[n * k : n * k + n]


def back(place, mine, other, weights):
    dims = (ROWS // 2, 3 * HID)
    return pl.pallas_call(
        back_kernel,
        grid_spec=pltpu.PrefetchScalarGridSpec(
            num_scalar_prefetch=1,
            grid=(HALF // WIDE,),
            in_specs=[whole(dims), whole(dims), *weight_specs()],
            out_specs=pl.BlockSpec((X, ROWS // 8, WIDE), lambda i, *_: (0, 0, i)),
            scratch_shapes=[pltpu.VMEM((2, *dims), BF16)],
        ),
        out_shape=shape((X, ROWS // 8, HALF), BF16),
        name="back",
    )(place, mine, other, *weights)


def grads_kernel(kept, place, mine, other, own, left, right, far_a, far_b, *refs):
    out, inner = refs[kept], refs[-1]

    @pl.when(pl.program_id(0) == 0)
    def _():
        is_mine = place[2] == (0 if kept else 1)
        both = jnp.where(is_mine, mine[...].astype(F32), other[...].astype(F32))
        low = iota((ROWS // 2, 2 * HID), 0) % 8 < 4
        pre = both[:, : 2 * HID]
        hid = both[:, 2 * HID :]
        zero = F32(0.0)
        first = jnp.where(low, pre, zero), jnp.where(low[:, :HID], zero, turned(hid))
        second = jnp.where(low, turned(pre), zero), jnp.where(low[:, :HID], zero, hid)
        for k, cols in ((0, pl.ds(0, 2 * HID)), (1, pl.ds(2 * HID, HID))):
            width = first[k].shape[1]
            pair = jnp.stack(
                [first[k].reshape(-1, 8, width), second[k].reshape(-1, 8, width)], axis=1
            )
            inner[:, cols] = pair.reshape(ROWS, width).astype(BF16)

    rows = jnp.concatenate([own[...], left[...], right[...], far_a[...], far_b[...]], axis=0)
    total = lax.dot_general(
        rows, inner[...], (((0,), (0,)), ((), ())), preferred_element_type=F32
    )

    def store(at, value):
        for i, near in enumerate(refs[1:4]):

            @pl.when(at == i)
            def _():
                near[...] = value.astype(BF16)

        for i, far in enumerate(refs[4:6]):

            @pl.when(at == 3)
            def _():
                far[...] = value[i * CUT // 2 : (i + 1) * CUT // 2].astype(BF16)

    for k in range(WIDE // CUT):
        part = total[k * CUT : (k + 1) * CUT]
        if kept:
            store(place[3 + pl.program_id(0) * (WIDE // CUT) + k], part + refs[0][k].astype(F32))
        else:
            out[k] = part.astype(BF16)


def grads(place, mine, other, blocks, received):
    dims = (ROWS // 2, 3 * HID)
    part = pl.BlockSpec((WIDE // CUT, CUT, 3 * HID), lambda i, *_: (i, 0, 0))
    cuts = [(n, 3 * HID) for n in (CUT, CUT, CUT, CUT // 2, CUT // 2)]
    return pl.pallas_call(
        functools.partial(grads_kernel, len(received)),
        grid_spec=pltpu.PrefetchScalarGridSpec(
            num_scalar_prefetch=1,
            grid=(HALF // WIDE,),
            in_specs=[whole(dims), whole(dims), *row_specs(), *[part for _ in received]],
            out_specs=[whole(dims) for dims in cuts] if received else part,
            scratch_shapes=[pltpu.VMEM((ROWS, 3 * HID), BF16)],
        ),
        out_shape=(
            [shape(dims, BF16) for dims in cuts]
            if received
            else shape((HALF // CUT, CUT, 3 * HID), BF16)
        ),
    )(place, mine, other, *blocks, *received)


def gathered(own, axis):
    half = own.shape[0] // 2
    left = lax.ppermute(own, axis, PLUS)
    right = lax.ppermute(own, axis, MINUS)
    far_a = lax.ppermute(left[:half], axis, PLUS)
    far_b = lax.ppermute(right[half:], axis, MINUS)
    return own, left, right, far_a, far_b


def scattered(parts):
    own, left, right, far_a, far_b = parts
    half = own.shape[0] // 2
    got_a = lax.ppermute(far_a, "y", MINUS).astype(F32)
    got_b = lax.ppermute(far_b, "y", PLUS).astype(F32)
    left = (left.astype(F32) + jnp.pad(got_a, ((0, half), (0, 0)))).astype(BF16)
    right = (right.astype(F32) + jnp.pad(got_b, ((half, 0), (0, 0)))).astype(BF16)
    left = lax.ppermute(left, "y", MINUS)
    right = lax.ppermute(right, "y", PLUS)
    return (own.astype(F32) + left.astype(F32) + right.astype(F32)).astype(BF16)


def work(latent, dout, routes, gate_w, norm_gain, w_gate_up, w_down):
    zp = lax.axis_index("z") % 2
    y = lax.axis_index("y")
    away = (jnp.arange(Y, dtype=jnp.int32) - y) % Y
    ring = jnp.where(away == 0, 0, jnp.where(away == 3, 1, away + 1))
    first = [zp, lax.axis_index("x"), (zp + lax.axis_index("c")) % 2]
    place = jnp.concatenate(
        [jnp.stack(first), ring, jnp.stack([(y + off) % Y for off in ORDER])]
    ).astype(jnp.int32)
    gain = norm_gain[None, :]
    routes = routes.T

    send, piece = send_rows(routes, gate_w.T, latent, dout, gain, w_gate_up, w_down)
    piece = lax.ppermute(piece, ("c", "z"), SWAP)
    got = lax.all_to_all(send, "z", 0, 0, tiled=True)
    joined = join(place, gathered(piece, "y"))
    weights = joined, lax.ppermute(joined, "c", TURN)
    blocks = gathered(got.reshape(ROWS // 4, HALF), "x")

    totals = []
    for some in (blocks[:3], blocks[3:]):
        mine, other = mix(place, some, weights)
        got = lax.ppermute(other, "z", FLIP)
        totals.append(mine + got.astype(F32))
    inner = gates(jnp.concatenate(totals, axis=0))
    outer = lax.ppermute(inner, "z", FLIP)

    sent = grads(place, inner, outer, blocks, ())
    received = lax.ppermute(sent, "c", TURN)
    part = back(place, inner, outer, weights)
    part = lax.all_to_all(part, "x", 0, 0, tiled=True)
    grad = scattered(grads(place, inner, outer, blocks, (received,)))
    grad = lax.ppermute(grad, ("c", "z"), SWAP)
    grad_gu = grad[:, : 2 * HID][None]
    grad_d = grad[:, 2 * HID :].T[None]

    summed = jnp.sum(part.astype(F32), axis=0).astype(BF16)
    home = lax.all_to_all(summed.reshape(Z, CAP, HALF), "z", 0, 0, tiled=True)
    return home_rows(routes, latent, gain, home), grad_gu, grad_d


def solution(mesh):
    fine = Mesh(mesh.devices.reshape(Y, C, Z, X), ("y", "c", "z", "x"))
    rows = P(("y", "c", "z", "x"), None)
    gate_up = P(("z", "x"), ("y", "c"), None)
    down = P(("z", "x"), None, ("y", "c"))
    return jax.shard_map(
        work,
        mesh=fine,
        in_specs=(rows, rows, rows, rows, P(), gate_up, down),
        out_specs=(rows, gate_up, down),
        check_vma=False,
    )
```

```python
import functools

import jax
import jax.numpy as jnp
from jax import lax
from jax.experimental import pallas as pl
from jax.experimental.pallas import tpu as pltpu
from jax.sharding import Mesh, PartitionSpec as P


CAP = 4
EPS = 1e-06
Y, C, Z, X = 4, 2, 16, 4
GROUPS = 8
HID = 128
D = 4096
HALF = D // 2
CUT = 512
WIDE = 2 * CUT
ROWS = 2 * Z * X * CAP
ROOM = pltpu.CompilerParams(vmem_limit_bytes=24 << 20)
F32 = jnp.float32
BF16 = jnp.bfloat16

SWAP = [
    (c * Z + 2 * e + p, p * Z + 2 * e + c) for c in range(C) for e in range(GROUPS) for p in range(2)
]
FLIP = [(i, i ^ 1) for i in range(Z)]
PLUS = [(i, (i + 1) % X) for i in range(X)]
MINUS = [(i, (i - 1) % X) for i in range(X)]
TURN = [(0, 1), (1, 0)]
ORDER = (0, 3, 1, 2)


def shape(dims, kind):
    return jax.ShapeDtypeStruct(dims, kind)


def iota(dims, axis):
    return lax.broadcasted_iota(jnp.int32, dims, axis)


def placing(routes):
    n = routes.shape[1]
    inside = routes < GROUPS
    chosen = jnp.sum(jnp.where(inside, routes, 0), axis=0, keepdims=True)
    present = jnp.sum(inside.astype(jnp.int32), axis=0, keepdims=True) > 0
    onehot = jnp.where((iota((GROUPS, n), 0) == chosen) & present, 1.0, 0.0)
    earlier = jnp.where(iota((n, n), 0) < iota((n, n), 1), 1.0, 0.0)
    rank = jnp.dot(onehot.astype(BF16), earlier.astype(BF16), preferred_element_type=F32)
    slot = jnp.sum(rank * onehot, axis=0, keepdims=True).astype(jnp.int32)
    return jnp.where(present, chosen * CAP + slot, -1)


def send_kernel(routes, gate_w, latent, dout, gain, gate_up, down, out, piece, held):
    piece[:, : 2 * HID] = gate_up[0]
    piece[:, 2 * HID :] = down[0].astype(F32).T.astype(BF16)
    n = routes.shape[1]
    where_to = placing(routes[...])
    weight = jnp.sum(
        jnp.where(routes[...] < GROUPS, gate_w[...], F32(0.0)), axis=0, keepdims=True
    )
    row = iota((2 * GROUPS * CAP, n), 0)
    hit = (row // 8 * CAP + row % CAP) == where_to
    take_in = hit & (row % 8 < CAP)
    take_dy = hit & (row % 8 >= CAP)
    factor = jnp.sum(jnp.where(take_dy, weight, F32(0.0)), axis=1, keepdims=True)
    take_in = jnp.where(take_in, 1.0, 0.0).astype(BF16)
    take_dy = jnp.where(take_dy, 1.0, 0.0).astype(BF16)
    square = jnp.zeros((2 * GROUPS * CAP, 1), F32)
    for d in range(D // CUT):
        cols = pl.ds(d * CUT, CUT)
        x = jnp.dot(take_in, latent[:, cols], preferred_element_type=F32)
        held[:, cols] = x
        square = square + jnp.sum(x * x, axis=1, keepdims=True)
    inverse = lax.rsqrt(square * (1.0 / D) + EPS)
    for d in range(D // CUT):
        cols = pl.ds(d * CUT, CUT)
        y = jnp.dot(take_dy, dout[:, cols], preferred_element_type=F32)
        value = held[:, cols] * inverse * gain[:, cols] + y * factor
        for e in range(GROUPS):
            out[2 * e + d % 2, :, pl.ds(d // 2 * CUT, CUT)] = value[8 * e : 8 * e + 8].astype(BF16)


def send_rows(*args):
    return pl.pallas_call(
        send_kernel,
        out_shape=[shape((Z, 8, HALF), BF16), shape((CUT, 3 * HID), BF16)],
        scratch_shapes=[pltpu.VMEM((2 * GROUPS * CAP, D), F32)],
        compiler_params=ROOM,
        name="send_rows",
    )(*args)


def join_kernel(place, own, left, right, far_a, far_b, out):
    half = CUT // 2
    for block, k, first in ((own, 0, 0), (left, 1, 0), (right, 2, 0), (far_a, 3, 0), (far_b, 3, half)):
        at = pl.multiple_of(place[7 + k] * CUT + first, half)
        out[pl.ds(at, block.shape[0]), :] = block[...]


def join(place, blocks):
    return pl.pallas_call(
        join_kernel,
        grid_spec=pltpu.PrefetchScalarGridSpec(
            num_scalar_prefetch=1,
            grid=(1,),
            in_specs=[whole(block.shape) for block in blocks],
            out_specs=whole((HALF, 3 * HID)),
        ),
        out_shape=shape((HALF, 3 * HID), BF16),
        compiler_params=ROOM,
        name="join",
    )(place, *blocks)


def home_kernel(routes, latent, gain, home, out, grad):
    n = routes.shape[1]
    where_to = placing(routes[...])
    take = jnp.where(iota((GROUPS * CAP, n), 0) == where_to, 1.0, 0.0).astype(BF16)
    for z in range(Z):
        for y in range(Y):
            cols = pl.ds((2 * y + z % 2) * CUT, CUT)
            grad[pl.ds(z // 2 * CAP, CAP), cols] = home[z, :, pl.ds(y * CUT, CUT)].astype(F32)
    x = jnp.dot(take, latent[...], preferred_element_type=F32)
    inverse = lax.rsqrt(jnp.sum(x * x, axis=1, keepdims=True) * (1.0 / D) + EPS)
    scaled = x * inverse
    g = grad[...] * gain[...]
    mean = jnp.sum(g * scaled, axis=1, keepdims=True) * (1.0 / D)
    value = (inverse * (g - scaled * mean)).astype(BF16)
    out[...] = lax.dot_general(
        take, value, (((0,), (0,)), ((), ())), preferred_element_type=F32
    ).astype(BF16)


def home_rows(routes, latent, gain, home):
    return pl.pallas_call(
        home_kernel,
        out_shape=shape(latent.shape, BF16),
        scratch_shapes=[pltpu.VMEM((GROUPS * CAP, D), F32)],
        compiler_params=ROOM,
        name="home_rows",
    )(routes, latent, gain, home)


def turned(value):
    n = value.shape[1]
    tiles = value.reshape(-1, 8, n)
    return pltpu.roll(tiles, 4, 1).reshape(-1, n)


def mix_kernel(count, place, *refs):
    blocks, weights = refs[:count], refs[count : count + 2]
    mine, other, total = refs[-3:]
    step = pl.program_id(0)
    rows = blocks[0][...]
    if count > 1:
        rows = jnp.concatenate([block[...] for block in blocks], axis=0)
    for g in range(2):
        part = jnp.dot(rows, weights[g][...], preferred_element_type=F32)

        @pl.when(step == 0)
        def _():
            total[g] = part

        @pl.when(step > 0)
        def _():
            total[g] = total[g] + part

    def packed(both):
        turns = both.reshape(-1, 2, 8, 3 * HID)
        first = turns[:, 0].reshape(-1, 3 * HID)
        second = turns[:, 1].reshape(-1, 3 * HID)
        low = iota((first.shape[0], 2 * HID), 0) % 8 < 4
        pre = jnp.where(low, first[:, : 2 * HID], turned(second[:, : 2 * HID]))
        dh = jnp.where(low[:, :HID], turned(first[:, 2 * HID :]), second[:, 2 * HID :])
        return pre, dh

    @pl.when(step == pl.num_programs(0) - 1)
    def _():
        pre, dh = packed(total[place[2]])
        mine[:, : 2 * HID] = pre
        mine[:, 2 * HID :] = dh
        pre, dh = packed(total[1 - place[2]])
        other[:, : 2 * HID] = pre.astype(BF16)
        other[:, 2 * HID :] = dh.astype(BF16)


def row_specs():
    return [
        pl.BlockSpec((n, WIDE), lambda i, *_: (0, i))
        for n in (ROWS // 4, ROWS // 4, ROWS // 4, ROWS // 8, ROWS // 8)
    ]


def weight_specs():
    return [pl.BlockSpec((WIDE, 3 * HID), lambda i, *_: (i, 0))] * 2


def whole(dims):
    return pl.BlockSpec(dims, lambda i, *_: (0,) * len(dims))


def mix(place, blocks, weights):
    rows = sum(block.shape[0] for block in blocks)
    dims = (rows // 2, 3 * HID)
    return pl.pallas_call(
        functools.partial(mix_kernel, len(blocks)),
        grid_spec=pltpu.PrefetchScalarGridSpec(
            num_scalar_prefetch=1,
            grid=(HALF // WIDE,),
            in_specs=[
                *[pl.BlockSpec((b.shape[0], WIDE), lambda i, *_: (0, i)) for b in blocks],
                *weight_specs(),
            ],
            out_specs=[whole(dims), whole(dims)],
            scratch_shapes=[pltpu.VMEM((2, rows, 3 * HID), F32)],
        ),
        out_shape=[shape(dims, F32), shape(dims, BF16)],
        compiler_params=ROOM,
    )(place, *blocks, *weights)


def gates(total):
    gate = total[:, :HID]
    up = total[:, HID : 2 * HID]
    dh = total[:, 2 * HID :]
    sig = jax.nn.sigmoid(gate)
    act = gate * sig
    d_gate = dh * up * sig * (1.0 + gate * (1.0 - sig))
    return jnp.concatenate([d_gate, dh * act, act * up], axis=1).astype(BF16)


def back_kernel(place, mine, other, weights_a, weights_b, out, inner):
    weights = weights_a, weights_b

    @pl.when(pl.program_id(0) == 0)
    def _():
        inner[place[2]] = mine[...]
        inner[1 - place[2]] = other[...]

    total = sum(
        lax.dot_general(
            inner[g, :, : 2 * HID],
            weights[g][:, : 2 * HID],
            (((1,), (1,)), ((), ())),
            preferred_element_type=F32,
        )
        for g in range(2)
    ).astype(BF16)
    n = ROWS // 8
    for k, off in enumerate(ORDER):
        out[lax.rem(place[1] + off, X)] = total[n * k : n * k + n]


def back(place, mine, other, weights):
    dims = (ROWS // 2, 3 * HID)
    return pl.pallas_call(
        back_kernel,
        grid_spec=pltpu.PrefetchScalarGridSpec(
            num_scalar_prefetch=1,
            grid=(HALF // WIDE,),
            in_specs=[whole(dims), whole(dims), *weight_specs()],
            out_specs=pl.BlockSpec((X, ROWS // 8, WIDE), lambda i, *_: (0, 0, i)),
            scratch_shapes=[pltpu.VMEM((2, *dims), BF16)],
        ),
        out_shape=shape((X, ROWS // 8, HALF), BF16),
        compiler_params=ROOM,
        name="back",
    )(place, mine, other, *weights)


def grads_kernel(kept, place, mine, other, own, left, right, far_a, far_b, *refs):
    out, inner = refs[kept], refs[-1]

    @pl.when(pl.program_id(0) == 0)
    def _():
        is_mine = place[2] == (0 if kept else 1)
        both = jnp.where(is_mine, mine[...].astype(F32), other[...].astype(F32))
        low = iota((ROWS // 2, 2 * HID), 0) % 8 < 4
        pre = both[:, : 2 * HID]
        hid = both[:, 2 * HID :]
        zero = F32(0.0)
        first = jnp.where(low, pre, zero), jnp.where(low[:, :HID], zero, turned(hid))
        second = jnp.where(low, turned(pre), zero), jnp.where(low[:, :HID], zero, hid)
        for k, cols in ((0, pl.ds(0, 2 * HID)), (1, pl.ds(2 * HID, HID))):
            width = first[k].shape[1]
            pair = jnp.stack(
                [first[k].reshape(-1, 8, width), second[k].reshape(-1, 8, width)], axis=1
            )
            inner[:, cols] = pair.reshape(ROWS, width).astype(BF16)

    rows = jnp.concatenate([own[...], left[...], right[...], far_a[...], far_b[...]], axis=0)
    total = lax.dot_general(
        rows, inner[...], (((0,), (0,)), ((), ())), preferred_element_type=F32
    )

    def store(at, value):
        for i, near in enumerate(refs[1:4]):

            @pl.when(at == i)
            def _():
                near[...] = value.astype(BF16)

        for i, far in enumerate(refs[4:6]):

            @pl.when(at == 3)
            def _():
                far[...] = value[i * CUT // 2 : (i + 1) * CUT // 2].astype(BF16)

    for k in range(WIDE // CUT):
        part = total[k * CUT : (k + 1) * CUT]
        if kept:
            store(place[3 + pl.program_id(0) * (WIDE // CUT) + k], part + refs[0][k].astype(F32))
        else:
            out[k] = part.astype(BF16)


def grads(place, mine, other, blocks, received):
    dims = (ROWS // 2, 3 * HID)
    part = pl.BlockSpec((WIDE // CUT, CUT, 3 * HID), lambda i, *_: (i, 0, 0))
    cuts = [(n, 3 * HID) for n in (CUT, CUT, CUT, CUT // 2, CUT // 2)]
    return pl.pallas_call(
        functools.partial(grads_kernel, len(received)),
        grid_spec=pltpu.PrefetchScalarGridSpec(
            num_scalar_prefetch=1,
            grid=(HALF // WIDE,),
            in_specs=[whole(dims), whole(dims), *row_specs(), *[part for _ in received]],
            out_specs=[whole(dims) for dims in cuts] if received else part,
            scratch_shapes=[pltpu.VMEM((ROWS, 3 * HID), BF16)],
        ),
        out_shape=(
            [shape(dims, BF16) for dims in cuts]
            if received
            else shape((HALF // CUT, CUT, 3 * HID), BF16)
        ),
        compiler_params=ROOM,
    )(place, mine, other, *blocks, *received)


def gathered(own, axis):
    half = own.shape[0] // 2
    left = lax.ppermute(own, axis, PLUS)
    right = lax.ppermute(own, axis, MINUS)
    far_a = lax.ppermute(left[:half], axis, PLUS)
    far_b = lax.ppermute(right[half:], axis, MINUS)
    return own, left, right, far_a, far_b


def scattered(parts):
    own, left, right, far_a, far_b = parts
    half = own.shape[0] // 2
    got_a = lax.ppermute(far_a, "y", MINUS).astype(F32)
    got_b = lax.ppermute(far_b, "y", PLUS).astype(F32)
    left = (left.astype(F32) + jnp.pad(got_a, ((0, half), (0, 0)))).astype(BF16)
    right = (right.astype(F32) + jnp.pad(got_b, ((half, 0), (0, 0)))).astype(BF16)
    left = lax.ppermute(left, "y", MINUS)
    right = lax.ppermute(right, "y", PLUS)
    return (own.astype(F32) + left.astype(F32) + right.astype(F32)).astype(BF16)


def work(latent, dout, routes, gate_w, norm_gain, w_gate_up, w_down):
    zp = lax.axis_index("z") % 2
    y = lax.axis_index("y")
    away = (jnp.arange(Y, dtype=jnp.int32) - y) % Y
    ring = jnp.where(away == 0, 0, jnp.where(away == 3, 1, away + 1))
    first = [zp, lax.axis_index("x"), (zp + lax.axis_index("c")) % 2]
    place = jnp.concatenate(
        [jnp.stack(first), ring, jnp.stack([(y + off) % Y for off in ORDER])]
    ).astype(jnp.int32)
    gain = norm_gain[None, :]
    routes = routes.T

    send, piece = send_rows(routes, gate_w.T, latent, dout, gain, w_gate_up, w_down)
    piece = lax.ppermute(piece, ("c", "z"), SWAP)
    got = lax.all_to_all(send, "z", 0, 0, tiled=True)
    joined = join(place, gathered(piece, "y"))
    weights = joined, lax.ppermute(joined, "c", TURN)
    blocks = gathered(got.reshape(ROWS // 4, HALF), "x")

    totals = []
    for some in (blocks[:3], blocks[3:]):
        mine, other = mix(place, some, weights)
        got = lax.ppermute(other, "z", FLIP)
        totals.append(mine + got.astype(F32))
    inner = gates(jnp.concatenate(totals, axis=0))
    outer = lax.ppermute(inner, "z", FLIP)

    sent = grads(place, inner, outer, blocks, ())
    received = lax.ppermute(sent, "c", TURN)
    part = back(place, inner, outer, weights)
    part = lax.all_to_all(part, "x", 0, 0, tiled=True)
    grad = scattered(grads(place, inner, outer, blocks, (received,)))
    grad = lax.ppermute(grad, ("c", "z"), SWAP)
    grad_gu = grad[:, : 2 * HID][None]
    grad_d = grad[:, 2 * HID :].T[None]

    summed = jnp.sum(part.astype(F32), axis=0).astype(BF16)
    home = lax.all_to_all(summed.reshape(Z, CAP, HALF), "z", 0, 0, tiled=True)
    return home_rows(routes, latent, gain, home), grad_gu, grad_d


def solution(mesh):
    fine = Mesh(mesh.devices.reshape(Y, C, Z, X), ("y", "c", "z", "x"))
    rows = P(("y", "c", "z", "x"), None)
    gate_up = P(("z", "x"), ("y", "c"), None)
    down = P(("z", "x"), None, ("y", "c"))
    return jax.shard_map(
        work,
        mesh=fine,
        in_specs=(rows, rows, rows, rows, P(), gate_up, down),
        out_specs=(rows, gate_up, down),
        check_vma=False,
    )
```
